512 devices in a mesh: shard: 128 (over y, z, core), tensor: 4 (over x).
Axes of the slice: x: 4, y: 8, z: 8, core: 2. Of those that a mesh axis runs over, the one named last changes fastest.
Arguments:
- grad_query: bfloat16 [128, 1024, 512], P('shard', None, 'tensor'), may hold values from -8 to 8
- error_query: float32 [128, 1024, 512], P('shard', None, 'tensor'), may hold values from -3 to 3
- grad_output: bfloat16 [128, 512, 1024], P('shard', 'tensor'), may hold values from -8 to 8
- error_output: float32 [128, 512, 1024], P('shard', 'tensor'), may hold values from -3 to 3
- start_query: float32 [512, 32], P('tensor'), may hold values from -6 to 6
- start_output: float32 [1024, 32], replicated, may hold values from -6 to 6
- weight_query: float32 [1024, 512], P('shard', 'tensor'), may hold values from -0.1875 to 0.1875
- weight_output: float32 [512, 1024], P('tensor', 'shard'), may hold values from -0.25 to 0.25
- moment_query: float32 [1024, 512], P('shard', 'tensor'), may hold values from -1.2 to 1.2
- moment_output: float32 [512, 1024], P('tensor', 'shard'), may hold values from -1.2 to 1.2
- grad_vector: bfloat16 [128, 3584], P('shard'), may hold values from -12 to 12
- moment_vector: float32 [3584], P('shard'), may hold values from -1.2 to 1.2
- weight_vector: float32 [3584], P('shard'), may hold values from 0.5 to 1.5
Outputs:
- new_error_query: float32 [128, 1024, 512], P('shard', None, 'tensor')
- new_error_output: float32 [128, 512, 1024], P('shard', 'tensor')
- new_moment_query: float32 [1024, 512], P('shard', 'tensor')
- new_moment_output: float32 [512, 1024], P('tensor', 'shard')
- new_weight_query: float32 [1024, 512], P(None, 'tensor')
- new_weight_output: float32 [512, 1024], P('tensor')
- new_moment_vector: float32 [3584], P('shard')
- new_weight_vector: float32 [3584], replicated
The draws below stay inside these ranges and needn't reach their ends.
All inputs are finite; a program needn't handle non-finite values.
Results may differ from the reference program's by a relative error of at most 0.0003.
Values sent between devices are 32-bit elements; how exact they have to be, the bound alone decides.
No kernel may reach another device: no remote copies, remote signals or barrier semaphores. Data moves between devices by JAX's collectives and lax.ppermute only.
A program may use at most 64 MiB of HBM per device.

```python
import jax
import jax.numpy as jnp
from jax import lax

D = 1024
RANK = 32
ROUNDS = 2
HW = 512
VEC = 3584
REPL = 128
N_SHARD = 128


def shared_gradient(key, replicas, height, breadth):
    common = jax.random.normal(jax.random.fold_in(key, 11), (height, breadth), jnp.float32)
    single = jax.random.normal(jax.random.fold_in(key, 12), (replicas, height, breadth), jnp.float32)
    return jnp.clip(common[None] + single, -8.0, 8.0)


def draw_grad_query(key, part):
    return shared_gradient(jax.random.fold_in(key, 1), REPL, D, HW).astype(jnp.bfloat16)


def draw_grad_output(key, part):
    return shared_gradient(jax.random.fold_in(key, 2), REPL, HW, D).astype(jnp.bfloat16)


def steps_of(key, shape, pieces, least, largest):
    factor_of, own = 1.0, jax.random.fold_in(key, 6)
    for position, parts in pieces:
        steps = jnp.exp(jax.random.uniform(jax.random.fold_in(own, position), (parts,), jnp.float32, least / len(pieces), largest / len(pieces)))
        factor_of = factor_of * jnp.repeat(steps, shape[position] // parts).reshape([-1 if axis == position else 1 for axis in range(len(shape))])
    return factor_of


def normal_values(rng, dims, width, limit, pieces=(), kind=jnp.bfloat16):
    array = width * jax.random.normal(rng, dims, jnp.float32)
    if pieces:
        array = array * steps_of(rng, dims, pieces, -0.22, 0.18)
    return jnp.clip(array, -limit, limit).astype(kind)


def setup_inputs(seed: int = 0) -> dict:
    key_of = jax.random.split(jax.random.key(seed), 14)
    grad_query = draw_grad_query(jax.random.fold_in(key_of[13], 71), 0)
    error_query = normal_values(key_of[1], (REPL, D, HW), 0.5, 3.0, ((0, 128), (2, 4)), jnp.float32)
    grad_output = draw_grad_output(jax.random.fold_in(key_of[13], 71), 0)
    error_output = normal_values(key_of[3], (REPL, HW, D), 0.5, 3.0, ((0, 128), (1, 4)), jnp.float32)
    start_query = normal_values(key_of[4], (HW, RANK), 1.0, 6.0, ((0, 4),), jnp.float32)
    start_output = normal_values(key_of[5], (D, RANK), 1.0, 6.0, (), jnp.float32)
    weight_query = normal_values(key_of[6], (D, HW), D ** -0.5, 0.1875, ((0, 128), (1, 4)), jnp.float32)
    weight_output = normal_values(key_of[7], (HW, D), HW ** -0.5, 0.25, ((0, 4), (1, 128)), jnp.float32)
    moment_query = normal_values(key_of[8], (D, HW), 0.2, 1.2, ((0, 128), (1, 4)), jnp.float32)
    moment_output = normal_values(key_of[9], (HW, D), 0.2, 1.2, ((0, 4), (1, 128)), jnp.float32)
    grad_vector = normal_values(key_of[10], (REPL, VEC), 2.0, 12.0, ((0, 128),))
    moment_vector = normal_values(key_of[11], (VEC,), 0.2, 1.2, ((0, 128),), jnp.float32)
    weight_vector = jnp.clip(1.0 + 0.1 * jax.random.normal(key_of[12], (VEC,), jnp.float32), 0.5, 1.5)
    return {"grad_query": grad_query, "error_query": error_query, "grad_output": grad_output, "error_output": error_output, "start_query": start_query, "start_output": start_output, "weight_query": weight_query, "weight_output": weight_output, "moment_query": moment_query, "moment_output": moment_output, "grad_vector": grad_vector, "moment_vector": moment_vector, "weight_vector": weight_vector}


def orthonormal(factor):
    gram = jnp.dot(factor.T.astype(jnp.float32), factor.astype(jnp.float32), precision=lax.Precision.HIGHEST, preferred_element_type=jnp.float32)
    lower = jnp.linalg.cholesky(gram)
    return jax.scipy.linalg.solve_triangular(lower, factor.T, lower=True).T

def reference(grad_query, error_query, grad_output, error_output, start_query, start_output, weight_query, weight_output, moment_query, moment_output, grad_vector, moment_vector, weight_vector):
    highest = lax.Precision.HIGHEST
    total_query = grad_query.astype(jnp.float32) + error_query
    total_output = grad_output.astype(jnp.float32) + error_output
    factor_query = start_query
    factor_output = start_output
    for turn in range(ROUNDS):
        left_query = orthonormal(jnp.einsum('rij,jk->ik', total_query, factor_query, precision=highest))
        factor_query = jnp.einsum('rij,ik->jk', total_query, left_query, precision=highest)
        left_output = orthonormal(jnp.einsum('rij,jk->ik', total_output, factor_output, precision=highest))
        factor_output = jnp.einsum('rij,ik->jk', total_output, left_output, precision=highest)
    approx_query = jnp.dot(left_query.astype(jnp.float32), factor_query.T.astype(jnp.float32), precision=highest, preferred_element_type=jnp.float32) / N_SHARD
    approx_output = jnp.dot(left_output.astype(jnp.float32), factor_output.T.astype(jnp.float32), precision=highest, preferred_element_type=jnp.float32) / N_SHARD
    new_error_query = total_query - approx_query[None]
    new_error_output = total_output - approx_output[None]
    new_moment_query = 0.9 * moment_query + approx_query
    new_moment_output = 0.9 * moment_output + approx_output
    new_weight_query = weight_query - 0.01 * new_moment_query
    new_weight_output = weight_output - 0.01 * new_moment_output
    vector_mean = jnp.sum(grad_vector.astype(jnp.float32), axis=0) / N_SHARD
    new_moment_vector = 0.9 * moment_vector + vector_mean
    new_weight_vector = weight_vector - 0.01 * new_moment_vector
    return (new_error_query, new_error_output, new_moment_query, new_moment_output, new_weight_query, new_weight_output, new_moment_vector, new_weight_vector)
```

```python
import jax
import jax.numpy as jnp
import numpy as np
from jax import lax
from jax.sharding import PartitionSpec as P

ROUNDS = 2
LANES = 128

highest = lax.Precision.HIGHEST


def dot(left, right, dims):
    return lax.dot_general(left, right, (dims, ((), ())), precision=highest, preferred_element_type=jnp.float32)


def ring_size(shards):
    ring = int(round((shards // 2) ** 0.5))
    assert 2 * ring * ring == shards
    return ring


def groups(ring):
    along_y = [[[(2 * (ring * y + z)) + c for y in range(ring)] for z in range(ring)] for c in range(2)]
    along_z = [[[(2 * (ring * y + z)) + c for z in range(ring)] for y in range(ring)] for c in range(2)]
    return along_y[0] + along_z[1], along_z[0] + along_y[1]


def swap_cores(value, shards):
    return lax.ppermute(value, "shard", [(s, s ^ 1) for s in range(shards)])


def exchange(value, group):
    return lax.all_to_all(value, "shard", 0, 0, axis_index_groups=group, tiled=True)


def share(value, group, size):
    return exchange(jnp.broadcast_to(value[None], (size, *value.shape)), group)


def inverse_lower(gram):
    lower = jnp.linalg.cholesky(gram)
    eye = jnp.eye(gram.shape[0], dtype=gram.dtype)
    return jax.scipy.linalg.solve_triangular(lower, eye, lower=True)


def local(
    grad_query,
    error_query,
    grad_output,
    error_output,
    start_query,
    start_output,
    weight_query,
    weight_output,
    moment_query,
    moment_output,
    grad_vector,
    moment_vector,
    weight_vector,
):
    shards = lax.axis_size("shard")
    tensors = lax.axis_size("tensor")
    index = lax.axis_index("shard")
    ring = ring_size(shards)
    first, second = groups(ring)
    even = (index % 2) == 0
    width = start_query.shape[0]
    height = start_output.shape[0]
    rank = start_query.shape[1]
    block = height // ring
    rows = height // shards
    vec = grad_vector.shape[1]
    piece = vec // ring
    small = vec // shards
    assert width == LANES and rows % 8 == 0 or rows * shards == height
    vec_rows = -(-piece // (8 * LANES)) * 8

    total_query = grad_query[0].astype(jnp.float32) + error_query[0]
    total_output = grad_output[0].astype(jnp.float32) + error_output[0]
    query_blocks = total_query.reshape(ring, block, width)
    output_blocks = total_output.reshape(width, ring, block).transpose(1, 0, 2)
    vector_blocks = jnp.pad(
        grad_vector[0].astype(jnp.float32).reshape(ring, piece), ((0, 0), (0, vec_rows * LANES - piece))
    ).reshape(ring, vec_rows, LANES)

    kept_query = weight_query - 0.009 * moment_query
    kept_output = (weight_output - 0.009 * moment_output).T
    kept_vector = jnp.pad(weight_vector - 0.009 * moment_vector, (0, LANES - small))

    mine = jnp.where(even, query_blocks, output_blocks)
    theirs = jnp.where(even, output_blocks, query_blocks)
    own_kept = jnp.where(even, kept_query, kept_output)
    other_kept = jnp.where(even, kept_output, kept_query)
    sent = jnp.concatenate([
        jnp.concatenate([theirs, vector_blocks], axis=1).reshape(-1, LANES),
        other_kept,
        jnp.pad(kept_vector[None], ((0, 7), (0, 0))),
    ])
    got = swap_cores(sent, shards)
    tall = ring * (block + vec_rows)
    summed = jnp.concatenate([mine, vector_blocks], axis=1) + got[:tall].reshape(ring, block + vec_rows, LANES)
    got_kept = got[tall:tall + rows]
    got_vector = got[tall + rows, :small]
    own_vector = kept_vector[:small]
    pair_kept = jnp.where(even, jnp.concatenate([own_kept, got_kept]), jnp.concatenate([got_kept, own_kept]))
    pair_vector = jnp.where(even, jnp.concatenate([own_vector, got_vector]), jnp.concatenate([got_vector, own_vector]))
    pair_vector = jnp.pad(pair_vector[None], ((0, 7), (0, LANES - 2 * small)))

    part = exchange(summed, first).sum(0)
    every = share(jnp.concatenate([part, pair_kept, pair_vector]), second, ring)
    whole = every[:, :block + vec_rows].sum(0)
    square = jnp.where(even, whole[:block], whole[:block].T)
    kept_rows = every[:, block + vec_rows:block + vec_rows + 2 * rows].reshape(block, LANES)
    kept_vectors = every[:, block + vec_rows + 2 * rows]
    every = share(jnp.concatenate([square, whole[block:], kept_rows, kept_vectors]), first, ring)
    matrix = every[:, :block].reshape(height, width)
    vector_sum = every[:, block:block + vec_rows].reshape(ring, -1)[:, :piece].reshape(vec)
    kept_all = every[:, block + vec_rows:2 * block + vec_rows].reshape(ring, ring, 2 * rows, LANES)
    kept_all = jnp.where(even, kept_all, kept_all.transpose(1, 0, 2, 3)).reshape(height, LANES)
    kept_vectors = every[:, 2 * block + vec_rows:][:, :, :2 * small]
    kept_vectors = jnp.where(even, kept_vectors, kept_vectors.transpose(1, 0, 2)).reshape(vec)
    kept_other = swap_cores(kept_all, shards)

    narrow = jnp.where(even, start_query.T, dot(start_output, matrix, ((0,), (0,))))
    for turn in range(ROUNDS):
        wide = dot(narrow, matrix, ((1,), (1,)))
        gram = jnp.pad(dot(narrow, narrow, ((1,), (1,))), ((0, 0), (0, LANES - rank)))
        sent = jnp.concatenate([wide, gram], axis=1)
        got = lax.all_to_all(jnp.broadcast_to(sent[None], (tensors, *sent.shape)), "tensor", 0, 0, tiled=True).sum(0)
        wide = got[:, :height]
        gram = jnp.where(even, dot(wide, wide, ((1,), (1,))), got[:, height:height + rank])
        inverse = inverse_lower(gram)
        wide = dot(inverse, wide, ((1,), (0,)))
        scaled = dot(inverse, narrow, ((1,), (0,)))
        narrow = dot(wide, matrix, ((1,), (0,)))
    mine = jnp.concatenate([wide, jnp.where(even, narrow, scaled)], axis=1)
    other = swap_cores(mine, shards)
    of_query = jnp.where(even, mine, other)
    of_output = jnp.where(even, other, mine)
    approx_query = dot(of_query[:, :height], of_query[:, height:], ((0,), (0,))) / shards
    approx_output = dot(of_output[:, height:], of_output[:, :height], ((0,), (0,))) / shards
    kept_query = jnp.where(even, kept_all, kept_other)
    kept_output = jnp.where(even, kept_other, kept_all).T

    new_error_query = (total_query - approx_query)[None]
    new_error_output = (total_output - approx_output)[None]
    block_query = lax.dynamic_slice_in_dim(approx_query, index * rows, rows, 0)
    block_output = lax.dynamic_slice_in_dim(approx_output, index * rows, rows, 1)
    new_moment_query = 0.9 * moment_query + block_query
    new_moment_output = 0.9 * moment_output + block_output
    new_weight_query = kept_query - 0.01 * approx_query
    new_weight_output = kept_output - 0.01 * approx_output
    vector_mean = vector_sum / shards
    new_moment_vector = 0.9 * moment_vector + lax.dynamic_slice_in_dim(vector_mean, index * small, small, 0)
    new_weight_vector = kept_vectors - 0.01 * vector_mean
    return (
        new_error_query,
        new_error_output,
        new_moment_query,
        new_moment_output,
        new_weight_query,
        new_weight_output,
        new_moment_vector,
        new_weight_vector,
    )


def solution(mesh):
    in_specs = (
        P("shard", None, "tensor"),
        P("shard", None, "tensor"),
        P("shard", "tensor", None),
        P("shard", "tensor", None),
        P("tensor", None),
        P(),
        P("shard", "tensor"),
        P("tensor", "shard"),
        P("shard", "tensor"),
        P("tensor", "shard"),
        P("shard", None),
        P("shard"),
        P("shard"),
    )
    out_specs = (
        P("shard", None, "tensor"),
        P("shard", "tensor", None),
        P("shard", "tensor"),
        P("tensor", "shard"),
        P(None, "tensor"),
        P("tensor", None),
        P("shard"),
        P(),
    )
    return jax.shard_map(local, mesh=mesh, in_specs=in_specs, out_specs=out_specs, check_vma=False)
```

```python
import functools

import jax
import jax.numpy as jnp
from jax import lax
from jax.experimental import pallas as pl
from jax.experimental.pallas import tpu as pltpu
from jax.sharding import PartitionSpec as P

ROUNDS = 2
LANES = 128

highest = lax.Precision.HIGHEST


def dot(left, right, dims):
    return lax.dot_general(left, right, (dims, ((), ())), precision=highest, preferred_element_type=jnp.float32)


def ring_size(shards):
    ring = int(round((shards // 2) ** 0.5))
    assert 2 * ring * ring == shards
    return ring


def groups(ring):
    along_y = [[[(2 * (ring * y + z)) + c for y in range(ring)] for z in range(ring)] for c in range(2)]
    along_z = [[[(2 * (ring * y + z)) + c for z in range(ring)] for y in range(ring)] for c in range(2)]
    return along_y[0] + along_z[1], along_z[0] + along_y[1]


def swap_cores(value, shards):
    return lax.ppermute(value, "shard", [(s, s ^ 1) for s in range(shards)])


def exchange(value, group):
    return lax.all_to_all(value, "shard", 0, 0, axis_index_groups=group, tiled=True)


def share(value, group, size):
    return exchange(jnp.broadcast_to(value[None], (size, *value.shape)), group)


def invert_lower(gram):
    rank = gram.shape[0]
    tiles = rank // 8
    half = LANES // 2
    lane = lax.broadcasted_iota(jnp.int32, (8, LANES), 1)
    sub = lax.broadcasted_iota(jnp.int32, (8, LANES), 0)
    rows = [
        jnp.where(lane < rank, gram[8 * t:8 * t + 8], jnp.where(lane == sub + (8 * t + half), 1.0, 0.0))
        for t in range(tiles)
    ]
    done = [jnp.zeros((8, LANES), jnp.float32) for _ in range(tiles)]
    for k in range(rank):
        at, place = k // 8, k % 8
        row = jnp.broadcast_to(rows[at][place:place + 1], (8, LANES))
        columns = [jnp.broadcast_to(rows[t][:, k:k + 1], (8, LANES)) for t in range(at, tiles)]
        pivot = jnp.broadcast_to(columns[0][place:place + 1], (8, LANES))
        scaled = row / pivot
        done[at] = jnp.where(sub == place, row * lax.rsqrt(pivot), done[at])
        for t in range(at, tiles):
            take = columns[t - at] * scaled
            rows[t] = rows[t] - (jnp.where(sub > place, take, 0.0) if t == at else take)
    return pltpu.roll(jnp.concatenate(done), half, 1)


def send_partials(narrow, recv, gram, sent, block):
    ring = recv.shape[0]
    rank = narrow.shape[0]
    gram[...] = jnp.zeros_like(gram)
    gram[:, :rank] = dot(narrow, narrow, ((1,), (1,)))
    own = gram[...]
    for copy in range(sent.shape[0]):
        sent[copy, :, ring * block:] = own
    for j in range(ring):
        part = dot(narrow, recv[j, :block], ((1,), (1,)))
        for copy in range(sent.shape[0]):
            sent[copy, :, j * block:(j + 1) * block] = part


def normalized(spot, got, gram, block, ring):
    rank = got.shape[1]
    total = got[0]
    for copy in range(1, got.shape[0]):
        total = total + got[copy]
    wide = total[:, :ring * block]
    gram[...] = total[:, ring * block:]

    @pl.when(spot[1] == 0)
    def _():
        gram[:, :rank] = dot(wide, wide, ((1,), (1,)))

    inverse = invert_lower(gram[...])[:, :rank]
    return inverse, dot(inverse, wide, ((1,), (0,)))


def times_matrix(wide, recv, block):
    return sum(dot(wide[:, j * block:(j + 1) * block], recv[j, :block], ((1,), (0,))) for j in range(recv.shape[0]))


def first_kernel(block, spot, recv, start_query, start_output, sent, narrow, gram):
    @pl.when(spot[1] == 0)
    def _():
        narrow[...] = start_query[...]

    @pl.when(spot[1] == 1)
    def _():
        narrow[...] = times_matrix(start_output[...], recv, block)

    send_partials(narrow[...], recv, gram, sent, block)


def middle_kernel(block, spot, recv, got, sent, narrow, gram):
    _, wide = normalized(spot, got, gram, block, recv.shape[0])
    value = times_matrix(wide, recv, block)
    narrow[...] = value
    send_partials(value, recv, gram, sent, block)


def last_kernel(block, spot, recv, got, narrow, factors, gram):
    ring = recv.shape[0]
    inverse, wide = normalized(spot, got, gram, block, ring)
    factors[:, :ring * block] = wide

    @pl.when(spot[1] == 0)
    def _():
        factors[:, ring * block:] = times_matrix(wide, recv, block)

    @pl.when(spot[1] == 1)
    def _():
        factors[:, ring * block:] = dot(inverse, narrow[...], ((1,), (0,)))


def final_kernel(
    block, shards, spot, mine, other, kept_mine, kept_other, grad_query, error_query, grad_output, error_output,
    moment_query, moment_output, new_error_query, new_error_output, new_moment_query, new_moment_output,
    new_weight_query, new_weight_output, error_q, error_o, weight_q, weight_o, sems,
):
    height, width = error_query.shape
    rows = moment_query.shape[0]
    scale = 1.0 / shards
    ring = height // block
    index = spot[0]

    def copies(j):
        down = pl.ds(j * block, block)
        return (
            pltpu.make_async_copy(error_q.at[down], new_error_query.at[down], sems.at[0, j]),
            pltpu.make_async_copy(weight_q.at[down], new_weight_query.at[down], sems.at[1, j]),
            pltpu.make_async_copy(error_o.at[:, down], new_error_output.at[:, down], sems.at[2, j]),
            pltpu.make_async_copy(weight_o.at[:, down], new_weight_output.at[:, down], sems.at[3, j]),
        )

    def body(query, output, kept_query, kept_output):
        right = query[:, height:] * scale
        left = output[:, height:] * scale
        for j in range(ring):
            down = slice(j * block, (j + 1) * block)
            approx = dot(query[:, down], right, ((0,), (0,)))
            error_q[down] = grad_query[down].astype(jnp.float32) + error_query[down] - approx
            weight_q[down] = kept_query[down] - 0.01 * approx
            approx = dot(left, output[:, down], ((0,), (0,)))
            error_o[:, down] = grad_output[:, down].astype(jnp.float32) + error_output[:, down] - approx
            weight_o[:, down] = kept_output[down] - 0.01 * approx
            for copy in copies(j):
                copy.start()
        along = index * rows
        base = pl.multiple_of(along // LANES * LANES, LANES)
        picked = pltpu.roll(query[:, pl.ds(base, LANES)], (LANES - along % LANES) % LANES, 1)
        new_moment_query[...] = 0.9 * moment_query[...] + dot(picked, right, ((0,), (0,)))[:rows]
        picked = pltpu.roll(output[:, pl.ds(base, LANES)], (LANES - along % LANES) % LANES, 1)
        new_moment_output[...] = 0.9 * moment_output[...] + dot(picked, left, ((0,), (0,)))[:rows]

    @pl.when(spot[1] == 0)
    def _():
        body(mine, other, kept_mine, kept_other)

    @pl.when(spot[1] == 1)
    def _():
        body(other, mine, kept_other, kept_mine)

    for j in range(ring):
        for copy in copies(j):
            copy.wait()


def shape(*dims):
    return jax.ShapeDtypeStruct(dims, jnp.float32)


def run(kernel, given, out_shape, scratch, out_specs=None, **options):
    whole = pl.BlockSpec(memory_space=pltpu.VMEM)
    specs = [pl.BlockSpec(memory_space=pltpu.SMEM)] + [whole] * (len(given) - 1)
    if out_specs is None:
        out_specs = jax.tree.map(lambda _: whole, out_shape)
    return pl.pallas_call(
        kernel, out_shape=out_shape, in_specs=specs, out_specs=out_specs, scratch_shapes=scratch,
        compiler_params=pltpu.CompilerParams(vmem_limit_bytes=40 * 2**20), **options,
    )(*given)


def local(
    grad_query,
    error_query,
    grad_output,
    error_output,
    start_query,
    start_output,
    weight_query,
    weight_output,
    moment_query,
    moment_output,
    grad_vector,
    moment_vector,
    weight_vector,
):
    shards = lax.axis_size("shard")
    tensors = lax.axis_size("tensor")
    index = lax.axis_index("shard")
    ring = ring_size(shards)
    first, second = groups(ring)
    even = (index % 2) == 0
    width = start_query.shape[0]
    height = start_output.shape[0]
    rank = start_query.shape[1]
    block = height // ring
    rows = height // shards
    vec = grad_vector.shape[1]
    piece = vec // ring
    small = vec // shards
    assert width == LANES and rows % 8 == 0 or rows * shards == height
    vec_rows = -(-piece // (8 * LANES)) * 8

    total_query = grad_query[0].astype(jnp.float32) + error_query[0]
    total_output = grad_output[0].astype(jnp.float32) + error_output[0]
    query_blocks = total_query.reshape(ring, block, width)
    output_blocks = total_output.reshape(width, ring, block).transpose(1, 0, 2)
    vector_blocks = jnp.pad(
        grad_vector[0].astype(jnp.float32).reshape(ring, piece), ((0, 0), (0, vec_rows * LANES - piece))
    ).reshape(ring, vec_rows, LANES)

    kept_query = weight_query - 0.009 * moment_query
    kept_output = (weight_output - 0.009 * moment_output).T
    kept_vector = jnp.pad(weight_vector - 0.009 * moment_vector, (0, LANES - small))

    mine = jnp.where(even, query_blocks, output_blocks)
    theirs = jnp.where(even, output_blocks, query_blocks)
    own_kept = jnp.where(even, kept_query, kept_output)
    other_kept = jnp.where(even, kept_output, kept_query)
    sent = jnp.concatenate([
        jnp.concatenate([theirs, vector_blocks], axis=1).reshape(-1, LANES),
        other_kept,
        jnp.pad(kept_vector[None], ((0, 7), (0, 0))),
    ])
    got = swap_cores(sent, shards)
    tall = ring * (block + vec_rows)
    summed = jnp.concatenate([mine, vector_blocks], axis=1) + got[:tall].reshape(ring, block + vec_rows, LANES)
    got_kept = got[tall:tall + rows]
    got_vector = got[tall + rows, :small]
    own_vector = kept_vector[:small]
    pair_kept = jnp.where(even, jnp.concatenate([own_kept, got_kept]), jnp.concatenate([got_kept, own_kept]))
    pair_vector = jnp.where(even, jnp.concatenate([own_vector, got_vector]), jnp.concatenate([got_vector, own_vector]))
    pair_vector = jnp.pad(pair_vector[None], ((0, 7), (0, LANES - 2 * small)))

    part = exchange(summed, first).sum(0)
    every = share(jnp.concatenate([part, pair_kept, pair_vector]), second, ring)
    whole = every[:, :block + vec_rows].sum(0)
    square = jnp.where(even, whole[:block], whole[:block].T)
    kept_rows = every[:, block + vec_rows:block + vec_rows + 2 * rows].reshape(block, LANES)
    kept_vectors = every[:, block + vec_rows + 2 * rows]
    every = share(jnp.concatenate([square, whole[block:], kept_rows, kept_vectors]), first, ring)
    vector_sum = every[:, block:block + vec_rows].reshape(ring, -1)[:, :piece].reshape(vec)
    kept_all = every[:, block + vec_rows:2 * block + vec_rows].reshape(ring, ring, 2 * rows, LANES)
    kept_turned = kept_all.transpose(1, 0, 2, 3).reshape(ring, block, LANES).transpose(0, 2, 1)
    kept_all = jnp.where(even, kept_all.reshape(ring, block, LANES), kept_turned).reshape(height, LANES)
    kept_vectors = every[:, 2 * block + vec_rows:][:, :, :2 * small]
    kept_vectors = jnp.where(even, kept_vectors, kept_vectors.transpose(1, 0, 2)).reshape(vec)
    kept_other = swap_cores(kept_all, shards)

    spot = jnp.stack([index, index % 2]).astype(jnp.int32)
    gram = pltpu.VMEM((rank, LANES), jnp.float32)
    partials = shape(tensors, rank, height + LANES)

    def gathered(value):
        return lax.all_to_all(value, "tensor", 0, 0, tiled=True)

    sent, narrow = run(
        functools.partial(first_kernel, block), (spot, every, start_query.T, start_output.T),
        (partials, shape(rank, width)), [gram],
    )
    for turn in range(ROUNDS - 1):
        sent, narrow = run(
            functools.partial(middle_kernel, block), (spot, every, gathered(sent)), (partials, shape(rank, width)), [gram]
        )
    mine = run(
        functools.partial(last_kernel, block), (spot, every, gathered(sent), narrow), shape(rank, height + width), [gram]
    )
    other = swap_cores(mine, shards)
    big = [pltpu.VMEM((height, width), jnp.float32), pltpu.VMEM((width, height), jnp.float32)]
    outside, within = pl.BlockSpec(memory_space=pl.ANY), pl.BlockSpec(memory_space=pltpu.VMEM)
    (
        new_error_query, new_error_output, new_moment_query, new_moment_output, new_weight_query, new_weight_output,
    ) = run(
        functools.partial(final_kernel, block, shards),
        (
            spot, mine, other, kept_all, kept_other, grad_query[0], error_query[0], grad_output[0], error_output[0],
            moment_query, moment_output.T,
        ),
        (shape(height, width), shape(width, height), shape(rows, width), shape(rows, width), shape(height, width), shape(width, height)),
        [big[0], big[1], big[0], big[1], pltpu.SemaphoreType.DMA((4, ring))],
        (outside, outside, within, within, outside, outside),
    )
    new_error_query = new_error_query[None]
    new_error_output = new_error_output[None]
    new_moment_output = new_moment_output.T
    vector_mean = vector_sum / shards
    new_moment_vector = 0.9 * moment_vector + lax.dynamic_slice_in_dim(vector_mean, index * small, small, 0)
    new_weight_vector = kept_vectors - 0.01 * vector_mean
    return (
        new_error_query,
        new_error_output,
        new_moment_query,
        new_moment_output,
        new_weight_query,
        new_weight_output,
        new_moment_vector,
        new_weight_vector,
    )


def solution(mesh):
    in_specs = (
        P("shard", None, "tensor"),
        P("shard", None, "tensor"),
        P("shard", "tensor", None),
        P("shard", "tensor", None),
        P("tensor", None),
        P(),
        P("shard", "tensor"),
        P("tensor", "shard"),
        P("shard", "tensor"),
        P("tensor", "shard"),
        P("shard", None),
        P("shard"),
        P("shard"),
    )
    out_specs = (
        P("shard", None, "tensor"),
        P("shard", "tensor", None),
        P("shard", "tensor"),
        P("tensor", "shard"),
        P(None, "tensor"),
        P("tensor", None),
        P("shard"),
        P(),
    )
    return jax.shard_map(local, mesh=mesh, in_specs=in_specs, out_specs=out_specs, check_vma=False)
```

```python
import functools

import jax
import jax.numpy as jnp
from jax import lax
from jax.experimental import pallas as pl
from jax.experimental.pallas import tpu as pltpu
from jax.sharding import PartitionSpec as P

ROUNDS = 2
LANES = 128

highest = lax.Precision.HIGHEST


def dot(left, right, dims):
    return lax.dot_general(left, right, (dims, ((), ())), precision=highest, preferred_element_type=jnp.float32)


def ring_size(shards):
    ring = int(round((shards // 2) ** 0.5))
    assert 2 * ring * ring == shards
    return ring


def groups(ring):
    along_y = [[[(2 * (ring * y + z)) + c for y in range(ring)] for z in range(ring)] for c in range(2)]
    along_z = [[[(2 * (ring * y + z)) + c for z in range(ring)] for y in range(ring)] for c in range(2)]
    return along_y[0] + along_z[1], along_z[0] + along_y[1]


def swap_cores(value, shards):
    return lax.ppermute(value, "shard", [(s, s ^ 1) for s in range(shards)])


def exchange(value, group):
    return lax.all_to_all(value, "shard", 0, 0, axis_index_groups=group, tiled=True)


def share(value, group, size):
    return exchange(jnp.broadcast_to(value[None], (size, *value.shape)), group)


def invert_lower(gram):
    rank = gram.shape[0]
    tiles = rank // 8
    half = LANES // 2
    lane = lax.broadcasted_iota(jnp.int32, (8, LANES), 1)
    sub = lax.broadcasted_iota(jnp.int32, (8, LANES), 0)
    rows = [
        jnp.where(lane < rank, gram[8 * t:8 * t + 8], jnp.where(lane == sub + (8 * t + half), 1.0, 0.0))
        for t in range(tiles)
    ]
    done = [jnp.zeros((8, LANES), jnp.float32) for _ in range(tiles)]
    wide = (8, LANES)
    for k in range(0, rank, 2):
        at, place = k // 8, k % 8
        near = [jnp.broadcast_to(rows[t][:, k:k + 1], wide) for t in range(at, tiles)]
        far = [jnp.broadcast_to(rows[t][:, k + 1:k + 2], wide) for t in range(at, tiles)]
        upper = jnp.broadcast_to(rows[at][place:place + 1], wide)
        lower = jnp.broadcast_to(rows[at][place + 1:place + 2], wide)
        pivot = jnp.broadcast_to(near[0][place:place + 1], wide)
        below = jnp.broadcast_to(near[0][place + 1:place + 2], wide)
        corner = jnp.broadcast_to(far[0][place + 1:place + 2], wide)
        inverse = 1.0 / pivot
        ratio = below * inverse
        second = corner - below * ratio
        lower = lower - ratio * upper
        done[at] = jnp.where(sub == place, upper * lax.rsqrt(pivot), done[at])
        done[at] = jnp.where(sub == place + 1, lower * lax.rsqrt(second), done[at])
        upper = upper * inverse
        lower = lower * (1.0 / second)
        for t in range(at, tiles):
            one, two = near[t - at], far[t - at]
            take = one * upper + (two - one * ratio) * lower
            rows[t] = rows[t] - (jnp.where(sub > place + 1, take, 0.0) if t == at else take)
    return pltpu.roll(jnp.concatenate(done), half, 1)


def send_partials(narrow, recv, stage, sent, sems, block):
    ring = recv.shape[0]
    rank = narrow.shape[0]
    stage[:, ring * block:] = jnp.zeros((rank, LANES), jnp.float32)
    stage[:, ring * block:ring * block + rank] = dot(narrow, narrow, ((1,), (1,)))
    for j in range(ring):
        stage[:, j * block:(j + 1) * block] = dot(narrow, recv[j, :block], ((1,), (1,)))
    copies = [pltpu.make_async_copy(stage, sent.at[peer], sems.at[peer]) for peer in range(sent.shape[0])]
    for copy in copies:
        copy.start()
    for copy in copies:
        copy.wait()


def normalized(spot, got, gram, block, ring):
    rank = got.shape[1]
    total = got[0]
    for copy in range(1, got.shape[0]):
        total = total + got[copy]
    wide = total[:, :ring * block]
    gram[...] = total[:, ring * block:]

    @pl.when(spot[1] == 0)
    def _():
        gram[:, :rank] = dot(wide, wide, ((1,), (1,)))

    inverse = invert_lower(gram[...])[:, :rank]
    return inverse, dot(inverse, wide, ((1,), (0,)))


def times_matrix(wide, recv, block):
    return sum(dot(wide[:, j * block:(j + 1) * block], recv[j, :block], ((1,), (0,))) for j in range(recv.shape[0]))


def first_kernel(block, spot, recv, start_query, start_output, sent, narrow, stage, sems):
    @pl.when(spot[1] == 0)
    def _():
        narrow[...] = start_query[...]

    @pl.when(spot[1] == 1)
    def _():
        narrow[...] = times_matrix(start_output[...], recv, block)

    send_partials(narrow[...], recv, stage, sent, sems, block)


def middle_kernel(block, spot, recv, got, sent, narrow, gram, stage, sems):
    _, wide = normalized(spot, got, gram, block, recv.shape[0])
    value = times_matrix(wide, recv, block)
    narrow[...] = value
    send_partials(value, recv, stage, sent, sems, block)


def last_kernel(block, spot, recv, got, narrow, factors, gram):
    ring = recv.shape[0]
    inverse, wide = normalized(spot, got, gram, block, ring)
    factors[:, :ring * block] = wide

    @pl.when(spot[1] == 0)
    def _():
        factors[:, ring * block:] = times_matrix(wide, recv, block)

    @pl.when(spot[1] == 1)
    def _():
        factors[:, ring * block:] = dot(inverse, narrow[...], ((1,), (0,)))


def final_kernel(
    block, shards, spot, mine, other, kept_mine, kept_other, grad_query, error_query, grad_output, error_output,
    moment_query, moment_output, new_error_query, new_error_output, new_moment_query, new_moment_output,
    new_weight_query, new_weight_output, error_q, error_o, weight_q, weight_o, sems,
):
    height, width = error_query.shape
    rows = moment_query.shape[0]
    scale = 1.0 / shards
    ring = height // block
    index = spot[0]

    def copies(j):
        down = pl.ds(j * block, block)
        return (
            pltpu.make_async_copy(error_q.at[down], new_error_query.at[down], sems.at[0, j]),
            pltpu.make_async_copy(weight_q.at[down], new_weight_query.at[down], sems.at[1, j]),
            pltpu.make_async_copy(error_o.at[:, down], new_error_output.at[:, down], sems.at[2, j]),
            pltpu.make_async_copy(weight_o.at[:, down], new_weight_output.at[:, down], sems.at[3, j]),
        )

    def body(query, output, kept_query, kept_output):
        right = query[:, height:] * scale
        left = output[:, height:] * scale
        for j in range(ring):
            down = slice(j * block, (j + 1) * block)
            approx = dot(query[:, down], right, ((0,), (0,)))
            error_q[down] = grad_query[down].astype(jnp.float32) + error_query[down] - approx
            weight_q[down] = kept_query[down] - 0.01 * approx
            approx = dot(left, output[:, down], ((0,), (0,)))
            error_o[:, down] = grad_output[:, down].astype(jnp.float32) + error_output[:, down] - approx
            weight_o[:, down] = kept_output[down] - 0.01 * approx
            for copy in copies(j):
                copy.start()
        along = index * rows
        base = pl.multiple_of(along // LANES * LANES, LANES)
        picked = pltpu.roll(query[:, pl.ds(base, LANES)], (LANES - along % LANES) % LANES, 1)
        new_moment_query[...] = 0.9 * moment_query[...] + dot(picked, right, ((0,), (0,)))[:rows]
        picked = pltpu.roll(output[:, pl.ds(base, LANES)], (LANES - along % LANES) % LANES, 1)
        new_moment_output[...] = 0.9 * moment_output[...] + dot(picked, left, ((0,), (0,)))[:rows]

    @pl.when(spot[1] == 0)
    def _():
        body(mine, other, kept_mine, kept_other)

    @pl.when(spot[1] == 1)
    def _():
        body(other, mine, kept_other, kept_mine)

    for j in range(ring):
        for copy in copies(j):
            copy.wait()


def prelude_kernel(
    ring, per, slot, vec, spot, grad_query, error_query, grad_output, error_output, grad_vector, weight_query,
    moment_query, weight_output, moment_output, weight_vector, moment_vector, mine, sent, kept,
    grad_q, error_q, grad_o, error_o, line, sems,
):
    height, width = grad_query.shape
    block = height // ring
    tall = block + slot
    rows = weight_query.shape[0]
    small = weight_vector.shape[1]
    index, odd = spot[0], spot[1]
    moves = [
        pltpu.make_async_copy(*pair, sems.at[n])
        for n, pair in enumerate(
            ((grad_query, grad_q), (error_query, error_q), (grad_output, grad_o), (error_output, error_o))
        )
    ]
    for move in moves:
        move.start()

    line[...] = jnp.zeros_like(line)
    line[0:1, :small] = weight_vector[...] - 0.009 * moment_vector[...]
    first = index * small
    spread = pltpu.roll(jnp.broadcast_to(line[0:1], (slot, LANES)), first % LANES, 1)
    sub = lax.broadcasted_iota(jnp.int32, (slot, LANES), 0)
    lane = lax.broadcasted_iota(jnp.int32, (slot, LANES), 1)
    for j in range(ring):
        after = LANES * (per * j + sub - per) + lane - first
        inside = (sub >= per) & (sub < 2 * per) & (after >= 0) & (after < small)
        value = jnp.where(inside, spread, 0.0)
        for ref in (mine, sent):
            ref[j * tall + block:(j + 1) * tall] = value
        for n in range(per):
            r = per * j + n
            if r * LANES < vec:
                row = grad_vector[:, r * LANES:(r + 1) * LANES].astype(jnp.float32)
                for ref in (mine, sent):
                    ref[j * tall + block + n:j * tall + block + n + 1] = row
    kept_query = weight_query[...] - 0.009 * moment_query[...]
    kept_output = weight_output[...] - 0.009 * moment_output[...]
    kept[...] = jnp.where(odd == 0, kept_query, kept_output)
    sent[ring * tall:ring * tall + rows] = jnp.where(odd == 0, kept_output, kept_query)

    def totals(query, output):
        moves[0].wait()
        moves[1].wait()
        for j in range(ring):
            down = slice(j * block, (j + 1) * block)
            query[j * tall:j * tall + block] = grad_q[down].astype(jnp.float32) + error_q[down]
        moves[2].wait()
        moves[3].wait()
        for j in range(ring):
            down = slice(j * block, (j + 1) * block)
            output[j * tall:j * tall + block] = grad_o[:, down].astype(jnp.float32) + error_o[:, down]

    @pl.when(odd == 0)
    def _():
        totals(mine, sent)

    @pl.when(odd == 1)
    def _():
        totals(sent, mine)


def vector_kernel(block, per, shards, spot, recv, moment_vector, new_moment, new_weight, mean, kept):
    ring = recv.shape[0]
    small = moment_vector.shape[1]
    for j in range(ring):
        mean[per * j:per * (j + 1)] = recv[j, block:block + per] * (1.0 / shards)
        kept[per * j:per * (j + 1)] = recv[j, block + per:block + 2 * per]
    mean[per * ring:] = jnp.zeros((mean.shape[0] - per * ring, LANES), jnp.float32)
    lines = new_weight.shape[0]
    new_weight[...] = kept[:lines] - 0.01 * mean[:lines]
    first = spot[0] * small
    row, off = first // LANES, first % LANES
    shift = (LANES - off) % LANES
    one = pltpu.roll(jnp.broadcast_to(mean[pl.ds(row, 1)], (8, LANES)), shift, 1)
    two = pltpu.roll(jnp.broadcast_to(mean[pl.ds(row + 1, 1)], (8, LANES)), shift, 1)
    lane = lax.broadcasted_iota(jnp.int32, (8, LANES), 1)
    own = jnp.where(lane < LANES - off, one, two)
    new_moment[...] = 0.9 * moment_vector[...] + own[0:1, :small]


def shape(*dims):
    return jax.ShapeDtypeStruct(dims, jnp.float32)


def run(kernel, given, out_shape, scratch, out_specs=None, outside=0, **options):
    whole = pl.BlockSpec(memory_space=pltpu.VMEM)
    left = [pl.BlockSpec(memory_space=pl.ANY)] * outside
    specs = [pl.BlockSpec(memory_space=pltpu.SMEM)] + left + [whole] * (len(given) - 1 - outside)
    if out_specs is None:
        out_specs = jax.tree.map(lambda _: whole, out_shape)
    return pl.pallas_call(
        kernel, out_shape=out_shape, in_specs=specs, out_specs=out_specs, scratch_shapes=scratch,
        compiler_params=pltpu.CompilerParams(vmem_limit_bytes=40 * 2**20), **options,
    )(*given)


def local(
    grad_query,
    error_query,
    grad_output,
    error_output,
    start_query,
    start_output,
    weight_query,
    weight_output,
    moment_query,
    moment_output,
    grad_vector,
    moment_vector,
    weight_vector,
):
    shards = lax.axis_size("shard")
    tensors = lax.axis_size("tensor")
    index = lax.axis_index("shard")
    ring = ring_size(shards)
    first, second = groups(ring)
    even = (index % 2) == 0
    width = start_query.shape[0]
    height = start_output.shape[0]
    rank = start_query.shape[1]
    block = height // ring
    rows = height // shards
    vec = grad_vector.shape[1]
    small = vec // shards
    lines = vec // LANES
    per = -(-lines // ring)
    slot = -(-2 * per // 8) * 8
    tall = block + slot
    assert width == LANES and rows * shards == height and small * shards == vec and lines * LANES == vec

    spot = jnp.stack([index, index % 2]).astype(jnp.int32)
    mine, sent, own_kept = run(
        functools.partial(prelude_kernel, ring, per, slot, vec),
        (
            spot, grad_query[0], error_query[0], grad_output[0], error_output[0], grad_vector, weight_query,
            moment_query, weight_output.T, moment_output.T, weight_vector[None], moment_vector[None],
        ),
        (shape(ring * tall, LANES), shape(ring * tall + rows, LANES), shape(rows, LANES)),
        [
            pltpu.VMEM((height, width), grad_query.dtype), pltpu.VMEM((height, width), jnp.float32),
            pltpu.VMEM((width, height), grad_output.dtype), pltpu.VMEM((width, height), jnp.float32),
            pltpu.VMEM((8, LANES), jnp.float32), pltpu.SemaphoreType.DMA((4,)),
        ],
        outside=4,
    )
    got = swap_cores(sent, shards)
    summed = (mine + got[:ring * tall]).reshape(ring, tall, LANES)
    got_kept = got[ring * tall:]
    pair_kept = jnp.where(even, jnp.concatenate([own_kept, got_kept]), jnp.concatenate([got_kept, own_kept]))

    part = exchange(summed, first).sum(0)
    every = share(jnp.concatenate([part, pair_kept]), second, ring)
    whole = every[:, :tall].sum(0)
    square = jnp.where(even, whole[:block], whole[:block].T)
    kept_rows = every[:, tall:].reshape(block, LANES)
    every = share(jnp.concatenate([square, whole[block:], kept_rows]), first, ring)
    kept_all = every[:, tall:].reshape(ring, ring, 2 * rows, LANES)
    kept_turned = kept_all.transpose(1, 0, 2, 3).reshape(ring, block, LANES).transpose(0, 2, 1)
    kept_all = jnp.where(even, kept_all.reshape(ring, block, LANES), kept_turned).reshape(height, LANES)
    kept_other = swap_cores(kept_all, shards)
    new_moment_vector, new_weight_vector = run(
        functools.partial(vector_kernel, block, per, shards), (spot, every, moment_vector[None]),
        (shape(1, small), shape(lines, LANES)),
        [pltpu.VMEM((per * ring + 8, LANES), jnp.float32), pltpu.VMEM((per * ring, LANES), jnp.float32)],
    )

    gram = pltpu.VMEM((rank, LANES), jnp.float32)
    partials = shape(tensors, rank, height + LANES)

    def gathered(value):
        return lax.all_to_all(value, "tensor", 0, 0, tiled=True)

    stage = [pltpu.VMEM((rank, height + LANES), jnp.float32), pltpu.SemaphoreType.DMA((tensors,))]
    outside, within = pl.BlockSpec(memory_space=pl.ANY), pl.BlockSpec(memory_space=pltpu.VMEM)
    sent, narrow = run(
        functools.partial(first_kernel, block), (spot, every, start_query.T, start_output.T),
        (partials, shape(rank, width)), stage, (outside, within),
    )
    for turn in range(ROUNDS - 1):
        sent, narrow = run(
            functools.partial(middle_kernel, block), (spot, every, gathered(sent)), (partials, shape(rank, width)),
            [gram, *stage], (outside, within),
        )
    mine = run(
        functools.partial(last_kernel, block), (spot, every, gathered(sent), narrow), shape(rank, height + width), [gram]
    )
    other = swap_cores(mine, shards)
    big = [pltpu.VMEM((height, width), jnp.float32), pltpu.VMEM((width, height), jnp.float32)]
    (
        new_error_query, new_error_output, new_moment_query, new_moment_output, new_weight_query, new_weight_output,
    ) = run(
        functools.partial(final_kernel, block, shards),
        (
            spot, mine, other, kept_all, kept_other, grad_query[0], error_query[0], grad_output[0], error_output[0],
            moment_query, moment_output.T,
        ),
        (shape(height, width), shape(width, height), shape(rows, width), shape(rows, width), shape(height, width), shape(width, height)),
        [big[0], big[1], big[0], big[1], pltpu.SemaphoreType.DMA((4, ring))],
        (outside, outside, within, within, outside, outside),
    )
    new_error_query = new_error_query[None]
    new_error_output = new_error_output[None]
    new_moment_output = new_moment_output.T
    return (
        new_error_query,
        new_error_output,
        new_moment_query,
        new_moment_output,
        new_weight_query,
        new_weight_output,
        new_moment_vector[0],
        new_weight_vector.reshape(vec),
    )


def solution(mesh):
    in_specs = (
        P("shard", None, "tensor"),
        P("shard", None, "tensor"),
        P("shard", "tensor", None),
        P("shard", "tensor", None),
        P("tensor", None),
        P(),
        P("shard", "tensor"),
        P("tensor", "shard"),
        P("shard", "tensor"),
        P("tensor", "shard"),
        P("shard", None),
        P("shard"),
        P("shard"),
    )
    out_specs = (
        P("shard", None, "tensor"),
        P("shard", "tensor", None),
        P("shard", "tensor"),
        P("tensor", "shard"),
        P(None, "tensor"),
        P("tensor", None),
        P("shard"),
        P(),
    )
    return jax.shard_map(local, mesh=mesh, in_specs=in_specs, out_specs=out_specs, check_vma=False)
```

```python
import functools

import jax
import jax.numpy as jnp
from jax import lax
from jax.experimental import pallas as pl
from jax.experimental.pallas import tpu as pltpu
from jax.sharding import PartitionSpec as P

ROUNDS = 2
LANES = 128

highest = lax.Precision.HIGHEST


def dot(left, right, dims):
    return lax.dot_general(left, right, (dims, ((), ())), precision=highest, preferred_element_type=jnp.float32)


def ring_size(shards):
    ring = int(round((shards // 2) ** 0.5))
    assert 2 * ring * ring == shards
    return ring


def groups(ring):
    along_y = [[[(2 * (ring * y + z)) + c for y in range(ring)] for z in range(ring)] for c in range(2)]
    along_z = [[[(2 * (ring * y + z)) + c for z in range(ring)] for y in range(ring)] for c in range(2)]
    return along_z[0] + along_y[1], along_y[0] + along_z[1]


def swap_cores(value, shards):
    return lax.ppermute(value, "shard", [(s, s ^ 1) for s in range(shards)])


def exchange(value, group):
    return lax.all_to_all(value, "shard", 0, 0, axis_index_groups=group, tiled=True)


def share(value, group, size):
    return exchange(jnp.broadcast_to(value[None], (size, *value.shape)), group)


def invert_lower(gram):
    rank = gram.shape[0]
    tiles = rank // 8
    half = LANES // 2
    lane = lax.broadcasted_iota(jnp.int32, (8, LANES), 1)
    sub = lax.broadcasted_iota(jnp.int32, (8, LANES), 0)
    rows = [
        jnp.where(lane < rank, gram[8 * t:8 * t + 8], jnp.where(lane == sub + (8 * t + half), 1.0, 0.0))
        for t in range(tiles)
    ]
    done = [jnp.zeros((8, LANES), jnp.float32) for _ in range(tiles)]
    wide = (8, LANES)
    for k in range(0, rank, 2):
        at, place = k // 8, k % 8
        near = [jnp.broadcast_to(rows[t][:, k:k + 1], wide) for t in range(at, tiles)]
        far = [jnp.broadcast_to(rows[t][:, k + 1:k + 2], wide) for t in range(at, tiles)]
        upper = jnp.broadcast_to(rows[at][place:place + 1], wide)
        lower = jnp.broadcast_to(rows[at][place + 1:place + 2], wide)
        pivot = jnp.broadcast_to(near[0][place:place + 1], wide)
        below = jnp.broadcast_to(near[0][place + 1:place + 2], wide)
        corner = jnp.broadcast_to(far[0][place + 1:place + 2], wide)
        inverse = 1.0 / pivot
        ratio = below * inverse
        second = corner - below * ratio
        lower = lower - ratio * upper
        done[at] = jnp.where(sub == place, upper * lax.rsqrt(pivot), done[at])
        done[at] = jnp.where(sub == place + 1, lower * lax.rsqrt(second), done[at])
        upper = upper * inverse
        lower = lower * (1.0 / second)
        for t in range(at, tiles):
            one, two = near[t - at], far[t - at]
            take = one * upper + (two - one * ratio) * lower
            rows[t] = rows[t] - (jnp.where(sub > place + 1, take, 0.0) if t == at else take)
    return pltpu.roll(jnp.concatenate(done), half, 1)


def send_partials(narrow, recv, stage, sent, sems, block):
    ring = recv.shape[0]
    rank = narrow.shape[0]
    stage[:, ring * block:] = jnp.zeros((rank, LANES), jnp.float32)
    stage[:, ring * block:ring * block + rank] = dot(narrow, narrow, ((1,), (1,)))
    for j in range(ring):
        stage[:, j * block:(j + 1) * block] = dot(narrow, recv[j, :block], ((1,), (1,)))
    copies = [pltpu.make_async_copy(stage, sent.at[peer], sems.at[peer]) for peer in range(sent.shape[0])]
    for copy in copies:
        copy.start()
    for copy in copies:
        copy.wait()


def normalized(spot, got, gram, block, ring):
    rank = got.shape[1]
    total = got[0]
    for copy in range(1, got.shape[0]):
        total = total + got[copy]
    wide = total[:, :ring * block]
    gram[...] = total[:, ring * block:]

    @pl.when(spot[1] == 0)
    def _():
        gram[:, :rank] = dot(wide, wide, ((1,), (1,)))

    inverse = invert_lower(gram[...])[:, :rank]
    return inverse, dot(inverse, wide, ((1,), (0,)))


def times_matrix(wide, recv, block):
    return sum(dot(wide[:, j * block:(j + 1) * block], recv[j, :block], ((1,), (0,))) for j in range(recv.shape[0]))


def first_kernel(block, spot, recv, start_query, start_output, sent, narrow, stage, sems):
    @pl.when(spot[1] == 0)
    def _():
        narrow[...] = start_query[...]

    @pl.when(spot[1] == 1)
    def _():
        narrow[...] = times_matrix(start_output[...], recv, block)

    send_partials(narrow[...], recv, stage, sent, sems, block)


def middle_kernel(block, spot, recv, got, sent, narrow, gram, stage, sems):
    _, wide = normalized(spot, got, gram, block, recv.shape[0])
    value = times_matrix(wide, recv, block)
    narrow[...] = value
    send_partials(value, recv, stage, sent, sems, block)


def last_kernel(block, spot, recv, got, narrow, factors, gram):
    ring = recv.shape[0]
    inverse, wide = normalized(spot, got, gram, block, ring)
    factors[:, :ring * block] = wide

    @pl.when(spot[1] == 0)
    def _():
        factors[:, ring * block:] = times_matrix(wide, recv, block)

    @pl.when(spot[1] == 1)
    def _():
        factors[:, ring * block:] = dot(inverse, narrow[...], ((1,), (0,)))


def final_kernel(
    block, shards, spot, mine, other, kept, grad_query, error_query, grad_output, error_output,
    moment_query, moment_output, new_error_query, new_error_output, new_moment_query, new_moment_output,
    new_weight_query, new_weight_output, error_q, error_o, weight_q, weight_o, sems,
):
    height, width = error_query.shape
    rows = moment_query.shape[0]
    scale = 1.0 / shards
    ring = height // block
    index = spot[0]

    def copies(j):
        down = pl.ds(j * block, block)
        return (
            pltpu.make_async_copy(error_q.at[down], new_error_query.at[down], sems.at[0, j]),
            pltpu.make_async_copy(weight_q.at[down], new_weight_query.at[down], sems.at[1, j]),
            pltpu.make_async_copy(error_o.at[:, down], new_error_output.at[:, down], sems.at[2, j]),
            pltpu.make_async_copy(weight_o.at[:, down], new_weight_output.at[:, down], sems.at[3, j]),
        )

    def body(query, output):
        right = query[:, height:] * scale
        left = output[:, height:] * scale
        for j in range(ring):
            down = slice(j * block, (j + 1) * block)
            old = kept[j * block // rows:(j + 1) * block // rows]
            approx = dot(query[:, down], right, ((0,), (0,)))
            error_q[down] = grad_query[down].astype(jnp.float32) + error_query[down] - approx
            weight_q[down] = old[:, :rows].reshape(block, width) - 0.01 * approx
            approx = dot(left, output[:, down], ((0,), (0,)))
            error_o[:, down] = grad_output[:, down].astype(jnp.float32) + error_output[:, down] - approx
            weight_o[:, down] = old[:, rows:].reshape(block, width).T - 0.01 * approx
            for copy in copies(j):
                copy.start()
        along = index * rows
        base = pl.multiple_of(along // LANES * LANES, LANES)
        picked = pltpu.roll(query[:, pl.ds(base, LANES)], (LANES - along % LANES) % LANES, 1)
        new_moment_query[...] = 0.9 * moment_query[...] + dot(picked, right, ((0,), (0,)))[:rows]
        picked = pltpu.roll(output[:, pl.ds(base, LANES)], (LANES - along % LANES) % LANES, 1)
        new_moment_output[...] = 0.9 * moment_output[...] + dot(picked, left, ((0,), (0,)))[:rows]

    @pl.when(spot[1] == 0)
    def _():
        body(mine, other)

    @pl.when(spot[1] == 1)
    def _():
        body(other, mine)

    for j in range(ring):
        for copy in copies(j):
            copy.wait()


def prelude_kernel(
    ring, per, slot, vec, spot, *refs
):
    far, (mine, sent), near, (line, sems) = refs[:7], refs[7:9], refs[9:16], refs[16:]
    moves = [pltpu.make_async_copy(*pair, sems.at[n]) for n, pair in enumerate(zip(far, near))]
    for move in moves:
        move.start()
    grad_q, error_q, grad_o, error_o, grad_vector, weight_vector, moment_vector = near
    height, width = grad_q.shape
    block = height // ring
    tall = block + slot
    small = weight_vector.shape[1]
    index, odd = spot[0], spot[1]
    for move in moves[4:]:
        move.wait()

    line[...] = jnp.zeros_like(line)
    line[0:1, :small] = weight_vector[...] - 0.009 * moment_vector[...]
    first = index * small
    spread = pltpu.roll(jnp.broadcast_to(line[0:1], (slot, LANES)), first % LANES, 1)
    sub = lax.broadcasted_iota(jnp.int32, (slot, LANES), 0)
    lane = lax.broadcasted_iota(jnp.int32, (slot, LANES), 1)
    for j in range(ring):
        after = LANES * (per * j + sub - per) + lane - first
        inside = (sub >= per) & (sub < 2 * per) & (after >= 0) & (after < small)
        value = jnp.where(inside, spread, 0.0)
        for ref in (mine, sent):
            ref[j * tall + block:(j + 1) * tall] = value
        for n in range(per):
            r = per * j + n
            if r * LANES < vec:
                row = grad_vector[:, r * LANES:(r + 1) * LANES].astype(jnp.float32)
                for ref in (mine, sent):
                    ref[j * tall + block + n:j * tall + block + n + 1] = row

    def totals(query, output):
        moves[0].wait()
        moves[1].wait()
        for j in range(ring):
            down = slice(j * block, (j + 1) * block)
            query[j * tall:j * tall + block] = grad_q[down].astype(jnp.float32) + error_q[down]
        moves[2].wait()
        moves[3].wait()
        for j in range(ring):
            down = slice(j * block, (j + 1) * block)
            output[j * tall:j * tall + block] = grad_o[:, down].astype(jnp.float32) + error_o[:, down]

    @pl.when(odd == 0)
    def _():
        totals(mine, sent)

    @pl.when(odd == 1)
    def _():
        totals(sent, mine)


def vector_kernel(block, per, shards, spot, recv, moment_vector, new_moment, new_weight, mean, kept):
    ring = recv.shape[0]
    small = moment_vector.shape[1]
    for j in range(ring):
        mean[per * j:per * (j + 1)] = recv[j, block:block + per] * (1.0 / shards)
        kept[per * j:per * (j + 1)] = recv[j, block + per:block + 2 * per]
    mean[per * ring:] = jnp.zeros((mean.shape[0] - per * ring, LANES), jnp.float32)
    lines = new_weight.shape[0]
    new_weight[...] = kept[:lines] - 0.01 * mean[:lines]
    first = spot[0] * small
    row, off = first // LANES, first % LANES
    shift = (LANES - off) % LANES
    one = pltpu.roll(jnp.broadcast_to(mean[pl.ds(row, 1)], (8, LANES)), shift, 1)
    two = pltpu.roll(jnp.broadcast_to(mean[pl.ds(row + 1, 1)], (8, LANES)), shift, 1)
    lane = lax.broadcasted_iota(jnp.int32, (8, LANES), 1)
    own = jnp.where(lane < LANES - off, one, two)
    new_moment[...] = 0.9 * moment_vector[...] + own[0:1, :small]


def shape(*dims):
    return jax.ShapeDtypeStruct(dims, jnp.float32)


def run(kernel, given, out_shape, scratch, out_specs=None, outside=0, **options):
    whole = pl.BlockSpec(memory_space=pltpu.VMEM)
    left = [pl.BlockSpec(memory_space=pltpu.HBM)] * outside
    specs = [pl.BlockSpec(memory_space=pltpu.SMEM)] + left + [whole] * (len(given) - 1 - outside)
    if out_specs is None:
        out_specs = jax.tree.map(lambda _: whole, out_shape)
    return pl.pallas_call(
        kernel, out_shape=out_shape, in_specs=specs, out_specs=out_specs, scratch_shapes=scratch,
        compiler_params=pltpu.CompilerParams(vmem_limit_bytes=40 * 2**20), **options,
    )(*given)


def local(
    grad_query,
    error_query,
    grad_output,
    error_output,
    start_query,
    start_output,
    weight_query,
    weight_output,
    moment_query,
    moment_output,
    grad_vector,
    moment_vector,
    weight_vector,
):
    shards = lax.axis_size("shard")
    tensors = lax.axis_size("tensor")
    index = lax.axis_index("shard")
    ring = ring_size(shards)
    first, second = groups(ring)
    asks = (index % 2) == 1
    width = start_query.shape[0]
    height = start_output.shape[0]
    rank = start_query.shape[1]
    block = height // ring
    rows = height // shards
    vec = grad_vector.shape[1]
    small = vec // shards
    lines = vec // LANES
    per = -(-lines // ring)
    slot = -(-2 * per // 8) * 8
    tall = block + slot
    assert width == LANES and rows * shards == height and small * shards == vec and lines * LANES == vec

    kept = jnp.concatenate([weight_query - 0.009 * moment_query, (weight_output - 0.009 * moment_output).T])
    kept = lax.all_gather(kept, "shard", axis=0, tiled=False)

    spot = jnp.stack([index, 1 - index % 2]).astype(jnp.int32)
    given = (
        grad_query[0], error_query[0], grad_output[0], error_output[0], grad_vector, weight_vector[None],
        moment_vector[None],
    )
    given = [pltpu.with_memory_space_constraint(value, pltpu.HBM) for value in given]
    mine, sent = run(
        functools.partial(prelude_kernel, ring, per, slot, vec), (spot, *given),
        (shape(ring * tall, LANES), shape(ring * tall, LANES)),
        [
            *(pltpu.VMEM(value.shape, value.dtype) for value in given),
            pltpu.VMEM((8, LANES), jnp.float32), pltpu.SemaphoreType.DMA((len(given),)),
        ],
        outside=len(given),
    )
    summed = (mine + swap_cores(sent, shards)).reshape(ring, tall, LANES)
    part = exchange(summed, first).sum(0)
    whole = share(part, second, ring).sum(0)
    square = jnp.where(asks, whole[:block], whole[:block].T)
    every = share(jnp.concatenate([square, whole[block:]]), first, ring)
    new_moment_vector, new_weight_vector = run(
        functools.partial(vector_kernel, block, per, shards), (spot, every, moment_vector[None]),
        (shape(1, small), shape(lines, LANES)),
        [pltpu.VMEM((per * ring + 8, LANES), jnp.float32), pltpu.VMEM((per * ring, LANES), jnp.float32)],
    )

    gram = pltpu.VMEM((rank, LANES), jnp.float32)
    partials = shape(tensors, rank, height + LANES)

    def gathered(value):
        return lax.all_to_all(value, "tensor", 0, 0, tiled=True)

    stage = [pltpu.VMEM((rank, height + LANES), jnp.float32), pltpu.SemaphoreType.DMA((tensors,))]
    outside, within = pl.BlockSpec(memory_space=pl.ANY), pl.BlockSpec(memory_space=pltpu.VMEM)
    sent, narrow = run(
        functools.partial(first_kernel, block), (spot, every, start_query.T, start_output.T),
        (partials, shape(rank, width)), stage, (outside, within),
    )
    for turn in range(ROUNDS - 1):
        sent, narrow = run(
            functools.partial(middle_kernel, block), (spot, every, gathered(sent)), (partials, shape(rank, width)),
            [gram, *stage], (outside, within),
        )
    got, new_moment_vector, new_weight_vector = lax.optimization_barrier(
        (gathered(sent), new_moment_vector, new_weight_vector)
    )
    mine = run(functools.partial(last_kernel, block), (spot, every, got, narrow), shape(rank, height + width), [gram])
    other = swap_cores(mine, shards)
    big = [pltpu.VMEM((height, width), jnp.float32), pltpu.VMEM((width, height), jnp.float32)]
    (
        new_error_query, new_error_output, new_moment_query, new_moment_output, new_weight_query, new_weight_output,
    ) = run(
        functools.partial(final_kernel, block, shards),
        (
            spot, mine, other, kept, grad_query[0], error_query[0], grad_output[0], error_output[0],
            moment_query, moment_output.T,
        ),
        (shape(height, width), shape(width, height), shape(rows, width), shape(rows, width), shape(height, width), shape(width, height)),
        [big[0], big[1], big[0], big[1], pltpu.SemaphoreType.DMA((4, ring))],
        (outside, outside, within, within, outside, outside),
    )
    new_error_query = new_error_query[None]
    new_error_output = new_error_output[None]
    new_moment_output = new_moment_output.T
    return (
        new_error_query,
        new_error_output,
        new_moment_query,
        new_moment_output,
        new_weight_query,
        new_weight_output,
        new_moment_vector[0],
        new_weight_vector.reshape(vec),
    )


def solution(mesh):
    in_specs = (
        P("shard", None, "tensor"),
        P("shard", None, "tensor"),
        P("shard", "tensor", None),
        P("shard", "tensor", None),
        P("tensor", None),
        P(),
        P("shard", "tensor"),
        P("tensor", "shard"),
        P("shard", "tensor"),
        P("tensor", "shard"),
        P("shard", None),
        P("shard"),
        P("shard"),
    )
    out_specs = (
        P("shard", None, "tensor"),
        P("shard", "tensor", None),
        P("shard", "tensor"),
        P("tensor", "shard"),
        P(None, "tensor"),
        P("tensor", None),
        P("shard"),
        P(),
    )
    return jax.shard_map(local, mesh=mesh, in_specs=in_specs, out_specs=out_specs, check_vma=False)
```

```python
import functools

import jax
import jax.numpy as jnp
from jax import lax
from jax.experimental import pallas as pl
from jax.experimental.pallas import tpu as pltpu
from jax.sharding import PartitionSpec as P

ROUNDS = 2
LANES = 128

highest = lax.Precision.HIGHEST


def dot(left, right, dims):
    return lax.dot_general(left, right, (dims, ((), ())), precision=highest, preferred_element_type=jnp.float32)


def ring_size(shards):
    ring = int(round((shards // 2) ** 0.5))
    assert 2 * ring * ring == shards
    return ring


def groups(ring):
    along_y = [[[(2 * (ring * y + z)) + c for y in range(ring)] for z in range(ring)] for c in range(2)]
    along_z = [[[(2 * (ring * y + z)) + c for z in range(ring)] for y in range(ring)] for c in range(2)]
    return along_z[0] + along_y[1], along_y[0] + along_z[1]


def swap_cores(value, shards):
    return lax.ppermute(value, "shard", [(s, s ^ 1) for s in range(shards)])


def exchange(value, group):
    return lax.all_to_all(value, "shard", 0, 0, axis_index_groups=group, tiled=True)


def share(value, group, size):
    return exchange(jnp.broadcast_to(value[None], (size, *value.shape)), group)


def invert_lower(gram):
    rank = gram.shape[0]
    tiles = rank // 8
    half = LANES // 2
    lane = lax.broadcasted_iota(jnp.int32, (8, LANES), 1)
    sub = lax.broadcasted_iota(jnp.int32, (8, LANES), 0)
    rows = [
        jnp.where(lane < rank, gram[8 * t:8 * t + 8], jnp.where(lane == sub + (8 * t + half), 1.0, 0.0))
        for t in range(tiles)
    ]
    done = [jnp.zeros((8, LANES), jnp.float32) for _ in range(tiles)]
    wide = (8, LANES)
    for k in range(0, rank, 2):
        at, place = k // 8, k % 8
        near = [jnp.broadcast_to(rows[t][:, k:k + 1], wide) for t in range(at, tiles)]
        far = [jnp.broadcast_to(rows[t][:, k + 1:k + 2], wide) for t in range(at, tiles)]
        upper = jnp.broadcast_to(rows[at][place:place + 1], wide)
        lower = jnp.broadcast_to(rows[at][place + 1:place + 2], wide)
        pivot = jnp.broadcast_to(near[0][place:place + 1], wide)
        below = jnp.broadcast_to(near[0][place + 1:place + 2], wide)
        corner = jnp.broadcast_to(far[0][place + 1:place + 2], wide)
        inverse = 1.0 / pivot
        ratio = below * inverse
        second = corner - below * ratio
        lower = lower - ratio * upper
        done[at] = jnp.where(sub == place, upper * lax.rsqrt(pivot), done[at])
        done[at] = jnp.where(sub == place + 1, lower * lax.rsqrt(second), done[at])
        upper = upper * inverse
        lower = lower * (1.0 / second)
        for t in range(at, tiles):
            one, two = near[t - at], far[t - at]
            take = one * upper + (two - one * ratio) * lower
            rows[t] = rows[t] - (jnp.where(sub > place + 1, take, 0.0) if t == at else take)
    return pltpu.roll(jnp.concatenate(done), half, 1)


def partials_of(narrow, recv, block, refs):
    ring = recv.shape[0]
    rank = narrow.shape[0]
    square = dot(narrow, narrow, ((1,), (1,)))
    for ref in refs:
        ref[:, ring * block:] = jnp.zeros((rank, LANES), jnp.float32)
        ref[:, ring * block:ring * block + rank] = square
    for j in range(ring):
        part = dot(narrow, recv[j, :block], ((1,), (1,)))
        for ref in refs:
            ref[:, j * block:(j + 1) * block] = part


def send_partials(narrow, recv, stage, sent, sems, block):
    partials_of(narrow, recv, block, [stage])
    copies = [pltpu.make_async_copy(stage, sent.at[peer], sems.at[peer]) for peer in range(sent.shape[0])]
    for copy in copies:
        copy.start()
    for copy in copies:
        copy.wait()


def normalized(spot, got, gram, block, ring):
    rank = got.shape[1]
    total = got[0]
    for copy in range(1, got.shape[0]):
        total = total + got[copy]
    wide = total[:, :ring * block]
    gram[...] = total[:, ring * block:]

    @pl.when(spot[1] == 0)
    def _():
        gram[:, :rank] = dot(wide, wide, ((1,), (1,)))

    inverse = invert_lower(gram[...])[:, :rank]
    return inverse, dot(inverse, wide, ((1,), (0,)))


def times_matrix(wide, recv, block):
    return sum(dot(wide[:, j * block:(j + 1) * block], recv[j, :block], ((1,), (0,))) for j in range(recv.shape[0]))


def first_kernel(block, spot, recv, start_query, start_output, sent, narrow, gram):
    @pl.when(spot[1] == 0)
    def _():
        narrow[...] = start_query[...]

    @pl.when(spot[1] == 1)
    def _():
        narrow[...] = times_matrix(start_output[...], recv, block)

    partials_of(narrow[...], recv, block, [sent.at[peer] for peer in range(sent.shape[0])])


def middle_kernel(block, spot, recv, got, sent, narrow, gram, stage, sems):
    _, wide = normalized(spot, got, gram, block, recv.shape[0])
    value = times_matrix(wide, recv, block)
    narrow[...] = value
    send_partials(value, recv, stage, sent, sems, block)


def last_kernel(block, spot, recv, got, narrow, factors, gram):
    ring = recv.shape[0]
    inverse, wide = normalized(spot, got, gram, block, ring)
    factors[:, :ring * block] = wide

    @pl.when(spot[1] == 0)
    def _():
        factors[:, ring * block:] = times_matrix(wide, recv, block)

    @pl.when(spot[1] == 1)
    def _():
        factors[:, ring * block:] = dot(inverse, narrow[...], ((1,), (0,)))


def final_kernel(
    block, shards, spot, mine, other, kept_mine, kept_other, grad_query, error_query, grad_output, error_output,
    moment_query, moment_output, new_error_query, new_error_output, new_moment_query, new_moment_output,
    new_weight_query, new_weight_output, error_q, error_o, weight_q, weight_o, sems,
):
    height, width = error_query.shape
    rows = moment_query.shape[0]
    scale = 1.0 / shards
    ring = height // block
    index = spot[0]

    def copies(j):
        down = pl.ds(j * block, block)
        return (
            pltpu.make_async_copy(error_q.at[down], new_error_query.at[down], sems.at[0, j]),
            pltpu.make_async_copy(weight_q.at[down], new_weight_query.at[down], sems.at[1, j]),
            pltpu.make_async_copy(error_o.at[:, down], new_error_output.at[:, down], sems.at[2, j]),
            pltpu.make_async_copy(weight_o.at[:, down], new_weight_output.at[:, down], sems.at[3, j]),
        )

    def body(query, output, kept_query, kept_output):
        right = query[:, height:] * scale
        left = output[:, height:] * scale
        for j in range(ring):
            down = slice(j * block, (j + 1) * block)
            approx = dot(query[:, down], right, ((0,), (0,)))
            error_q[down] = grad_query[down].astype(jnp.float32) + error_query[down] - approx
            weight_q[down] = kept_query[down] - 0.01 * approx
            approx = dot(left, output[:, down], ((0,), (0,)))
            error_o[:, down] = grad_output[:, down].astype(jnp.float32) + error_output[:, down] - approx
            weight_o[:, down] = kept_output[down] - 0.01 * approx
            for copy in copies(j):
                copy.start()
        along = index * rows
        base = pl.multiple_of(along // LANES * LANES, LANES)
        picked = pltpu.roll(query[:, pl.ds(base, LANES)], (LANES - along % LANES) % LANES, 1)
        new_moment_query[...] = 0.9 * moment_query[...] + dot(picked, right, ((0,), (0,)))[:rows]
        picked = pltpu.roll(output[:, pl.ds(base, LANES)], (LANES - along % LANES) % LANES, 1)
        new_moment_output[...] = 0.9 * moment_output[...] + dot(picked, left, ((0,), (0,)))[:rows]

    @pl.when(spot[1] == 0)
    def _():
        body(mine, other, kept_mine, kept_other)

    @pl.when(spot[1] == 1)
    def _():
        body(other, mine, kept_other, kept_mine)

    for j in range(ring):
        for copy in copies(j):
            copy.wait()


def prelude_kernel(ring, per, slot, vec, spot, *refs):
    far, total, near, (line, sems) = refs[:11], refs[11], refs[12:23], refs[23:]
    moves = [pltpu.make_async_copy(*pair, sems.at[n]) for n, pair in enumerate(zip(far, near))]
    grad_q, error_q, grad_o, error_o, grad_vector, weight_query, moment_query, weight_output, moment_output = near[:9]
    weight_vector, moment_vector = near[9:]
    height, width = grad_q.shape
    block = height // ring
    tall = block + slot
    rows = weight_query.shape[0]
    small = weight_vector.shape[1]
    index, which = spot[0], spot[1]

    @pl.when(which == 0)
    def _():
        moves[0].start()
        moves[1].start()

    @pl.when(which == 1)
    def _():
        moves[2].start()
        moves[3].start()

    for move in moves[4:]:
        move.start()
    for move in moves[4:]:
        move.wait()
    line[...] = jnp.zeros_like(line)
    line[0:1, :small] = weight_vector[...] - 0.009 * moment_vector[...]
    first = index * small
    spread = pltpu.roll(jnp.broadcast_to(line[0:1], (slot, LANES)), first % LANES, 1)
    sub = lax.broadcasted_iota(jnp.int32, (slot, LANES), 0)
    lane = lax.broadcasted_iota(jnp.int32, (slot, LANES), 1)
    for j in range(ring):
        after = LANES * (per * j + sub - per) + lane - first
        inside = (sub >= per) & (sub < 2 * per) & (after >= 0) & (after < small)
        total[j * tall + block:(j + 1) * tall] = jnp.where(inside, spread, 0.0)
        for n in range(per):
            r = per * j + n
            if r * LANES < vec:
                row = grad_vector[:, r * LANES:(r + 1) * LANES].astype(jnp.float32)
                total[j * tall + block + n:j * tall + block + n + 1] = row

    @pl.when(which == 0)
    def _():
        total[ring * tall:] = weight_query[...] - 0.009 * moment_query[...]
        moves[0].wait()
        moves[1].wait()
        for j in range(ring):
            down = slice(j * block, (j + 1) * block)
            total[j * tall:j * tall + block] = grad_q[down].astype(jnp.float32) + error_q[down]

    @pl.when(which == 1)
    def _():
        total[ring * tall:] = weight_output[...] - 0.009 * moment_output[...]
        moves[2].wait()
        moves[3].wait()
        for j in range(ring):
            down = slice(j * block, (j + 1) * block)
            total[j * tall:j * tall + block] = grad_o[:, down].astype(jnp.float32) + error_o[:, down]


def vector_kernel(block, per, shards, spot, recv, moment_vector, new_moment, new_weight, mean, kept):
    ring = recv.shape[0]
    small = moment_vector.shape[1]
    for j in range(ring):
        mean[per * j:per * (j + 1)] = recv[j, block:block + per] * (1.0 / shards)
        kept[per * j:per * (j + 1)] = recv[j, block + per:block + 2 * per]
    mean[per * ring:] = jnp.zeros((mean.shape[0] - per * ring, LANES), jnp.float32)
    lines = new_weight.shape[0]
    new_weight[...] = kept[:lines] - 0.01 * mean[:lines]
    first = spot[0] * small
    row, off = first // LANES, first % LANES
    shift = (LANES - off) % LANES
    one = pltpu.roll(jnp.broadcast_to(mean[pl.ds(row, 1)], (8, LANES)), shift, 1)
    two = pltpu.roll(jnp.broadcast_to(mean[pl.ds(row + 1, 1)], (8, LANES)), shift, 1)
    lane = lax.broadcasted_iota(jnp.int32, (8, LANES), 1)
    own = jnp.where(lane < LANES - off, one, two)
    new_moment[...] = 0.9 * moment_vector[...] + own[0:1, :small]


def shape(*dims):
    return jax.ShapeDtypeStruct(dims, jnp.float32)


def run(kernel, given, out_shape, scratch, out_specs=None, outside=0, **options):
    whole = pl.BlockSpec(memory_space=pltpu.VMEM)
    left = [pl.BlockSpec(memory_space=pltpu.HBM)] * outside
    specs = [pl.BlockSpec(memory_space=pltpu.SMEM)] + left + [whole] * (len(given) - 1 - outside)
    if out_specs is None:
        out_specs = jax.tree.map(lambda _: whole, out_shape)
    return pl.pallas_call(
        kernel, out_shape=out_shape, in_specs=specs, out_specs=out_specs, scratch_shapes=scratch,
        compiler_params=pltpu.CompilerParams(vmem_limit_bytes=40 * 2**20), **options,
    )(*given)


def local(
    grad_query,
    error_query,
    grad_output,
    error_output,
    start_query,
    start_output,
    weight_query,
    weight_output,
    moment_query,
    moment_output,
    grad_vector,
    moment_vector,
    weight_vector,
):
    shards = lax.axis_size("shard")
    tensors = lax.axis_size("tensor")
    index = lax.axis_index("shard")
    ring = ring_size(shards)
    first, second = groups(ring)
    asks = (index % 2) == 1
    width = start_query.shape[0]
    height = start_output.shape[0]
    rank = start_query.shape[1]
    block = height // ring
    rows = height // shards
    vec = grad_vector.shape[1]
    small = vec // shards
    lines = vec // LANES
    per = -(-lines // ring)
    slot = -(-2 * per // 8) * 8
    tall = block + slot
    assert width == LANES and rows * shards == height and small * shards == vec and lines * LANES == vec

    spot = jnp.stack([index, 1 - index % 2]).astype(jnp.int32)
    given = (
        grad_query[0], error_query[0], grad_output[0], error_output[0], grad_vector, weight_query, moment_query,
        weight_output.T, moment_output.T, weight_vector[None], moment_vector[None],
    )
    given = [pltpu.with_memory_space_constraint(value, pltpu.HBM) for value in given]

    def prelude(spot):
        return run(
            functools.partial(prelude_kernel, ring, per, slot, vec), (spot, *given), shape(ring * tall + rows, LANES),
            [
                *(pltpu.VMEM(value.shape, value.dtype) for value in given),
                pltpu.VMEM((8, LANES), jnp.float32), pltpu.SemaphoreType.DMA((len(given),)),
            ],
            outside=len(given),
        )

    got = swap_cores(prelude(jnp.stack([index, index % 2]).astype(jnp.int32)), shards)
    mine = prelude(spot)
    summed = (mine[:ring * tall] + got[:ring * tall]).reshape(ring, tall, LANES)
    own_kept, got_kept = mine[ring * tall:], got[ring * tall:]
    pair_kept = jnp.where(asks, jnp.concatenate([got_kept, own_kept]), jnp.concatenate([own_kept, got_kept]))

    part = exchange(summed, first).sum(0)
    every = share(jnp.concatenate([part, pair_kept]), second, ring)
    whole = every[:, :tall].sum(0)
    square = jnp.where(asks, whole[:block], whole[:block].T)
    kept_rows = every[:, tall:].reshape(block, LANES)
    every = share(jnp.concatenate([square, whole[block:], kept_rows]), first, ring)

    gram = pltpu.VMEM((rank, LANES), jnp.float32)
    partials = shape(tensors, rank, height + LANES)

    def gathered(value):
        return lax.all_to_all(value, "tensor", 0, 0, tiled=True)

    stage = [pltpu.VMEM((rank, height + LANES), jnp.float32), pltpu.SemaphoreType.DMA((tensors,))]
    outside, within = pl.BlockSpec(memory_space=pl.ANY), pl.BlockSpec(memory_space=pltpu.VMEM)
    sent, narrow = run(
        functools.partial(first_kernel, block), (spot, every, start_query.T, start_output.T),
        (partials, shape(rank, width)), [gram],
    )
    for turn in range(ROUNDS - 1):
        sent, narrow = run(
            functools.partial(middle_kernel, block), (spot, every, gathered(sent)), (partials, shape(rank, width)),
            [gram, *stage], (outside, within),
        )

    sent, every = lax.optimization_barrier((sent, every))
    kept_all = every[:, tall:].reshape(ring, ring, 2 * rows, LANES)
    kept_turned = kept_all.transpose(1, 0, 2, 3).reshape(ring, block, LANES).transpose(0, 2, 1)
    kept_all = jnp.where(asks, kept_all.reshape(ring, block, LANES), kept_turned).reshape(height, LANES)
    kept_other = swap_cores(kept_all, shards)
    new_moment_vector, new_weight_vector = run(
        functools.partial(vector_kernel, block, per, shards), (spot, every, moment_vector[None]),
        (shape(1, small), shape(lines, LANES)),
        [pltpu.VMEM((per * ring + 8, LANES), jnp.float32), pltpu.VMEM((per * ring, LANES), jnp.float32)],
    )
    got, new_moment_vector, new_weight_vector = lax.optimization_barrier(
        (gathered(sent), new_moment_vector, new_weight_vector)
    )
    mine = run(functools.partial(last_kernel, block), (spot, every, got, narrow), shape(rank, height + width), [gram])
    other = swap_cores(mine, shards)
    big = [pltpu.VMEM((height, width), jnp.float32), pltpu.VMEM((width, height), jnp.float32)]
    (
        new_error_query, new_error_output, new_moment_query, new_moment_output, new_weight_query, new_weight_output,
    ) = run(
        functools.partial(final_kernel, block, shards),
        (
            spot, mine, other, kept_all, kept_other, grad_query[0], error_query[0], grad_output[0], error_output[0],
            moment_query, moment_output.T,
        ),
        (shape(height, width), shape(width, height), shape(rows, width), shape(rows, width), shape(height, width), shape(width, height)),
        [big[0], big[1], big[0], big[1], pltpu.SemaphoreType.DMA((4, ring))],
        (outside, outside, within, within, outside, outside),
    )
    new_error_query = new_error_query[None]
    new_error_output = new_error_output[None]
    new_moment_output = new_moment_output.T
    return (
        new_error_query,
        new_error_output,
        new_moment_query,
        new_moment_output,
        new_weight_query,
        new_weight_output,
        new_moment_vector[0],
        new_weight_vector.reshape(vec),
    )


def solution(mesh):
    in_specs = (
        P("shard", None, "tensor"),
        P("shard", None, "tensor"),
        P("shard", "tensor", None),
        P("shard", "tensor", None),
        P("tensor", None),
        P(),
        P("shard", "tensor"),
        P("tensor", "shard"),
        P("shard", "tensor"),
        P("tensor", "shard"),
        P("shard", None),
        P("shard"),
        P("shard"),
    )
    out_specs = (
        P("shard", None, "tensor"),
        P("shard", "tensor", None),
        P("shard", "tensor"),
        P("tensor", "shard"),
        P(None, "tensor"),
        P("tensor", None),
        P("shard"),
        P(),
    )
    return jax.shard_map(local, mesh=mesh, in_specs=in_specs, out_specs=out_specs, check_vma=False)
```

```python
import functools

import jax
import jax.numpy as jnp
from jax import lax
from jax.experimental import pallas as pl
from jax.experimental.pallas import tpu as pltpu
from jax.sharding import PartitionSpec as P

ROUNDS = 2
LANES = 128

highest = lax.Precision.HIGHEST


def dot(left, right, dims):
    return lax.dot_general(left, right, (dims, ((), ())), precision=highest, preferred_element_type=jnp.float32)


def ring_size(shards):
    ring = int(round((shards // 2) ** 0.5))
    assert 2 * ring * ring == shards
    return ring


def groups(ring):
    along_y = [[[(2 * (ring * y + z)) + c for y in range(ring)] for z in range(ring)] for c in range(2)]
    along_z = [[[(2 * (ring * y + z)) + c for z in range(ring)] for y in range(ring)] for c in range(2)]
    return along_z[0] + along_y[1], along_y[0] + along_z[1]


def swap_cores(value, shards):
    return lax.ppermute(value, "shard", [(s, s ^ 1) for s in range(shards)])


def exchange(value, group):
    return lax.all_to_all(value, "shard", 0, 0, axis_index_groups=group, tiled=True)


def share(value, group, size):
    return exchange(jnp.broadcast_to(value[None], (size, *value.shape)), group)


def invert_lower(gram):
    rank = gram.shape[0]
    tiles = rank // 8
    half = LANES // 2
    lane = lax.broadcasted_iota(jnp.int32, (8, LANES), 1)
    sub = lax.broadcasted_iota(jnp.int32, (8, LANES), 0)
    rows = [
        jnp.where(lane < rank, gram[8 * t:8 * t + 8], jnp.where(lane == sub + (8 * t + half), 1.0, 0.0))
        for t in range(tiles)
    ]
    done = [jnp.zeros((8, LANES), jnp.float32) for _ in range(tiles)]
    wide = (8, LANES)
    for k in range(0, rank, 2):
        at, place = k // 8, k % 8
        near = [jnp.broadcast_to(rows[t][:, k:k + 1], wide) for t in range(at, tiles)]
        far = [jnp.broadcast_to(rows[t][:, k + 1:k + 2], wide) for t in range(at, tiles)]
        upper = jnp.broadcast_to(rows[at][place:place + 1], wide)
        lower = jnp.broadcast_to(rows[at][place + 1:place + 2], wide)
        pivot = jnp.broadcast_to(near[0][place:place + 1], wide)
        below = jnp.broadcast_to(near[0][place + 1:place + 2], wide)
        corner = jnp.broadcast_to(far[0][place + 1:place + 2], wide)
        inverse = 1.0 / pivot
        ratio = below * inverse
        second = corner - below * ratio
        lower = lower - ratio * upper
        done[at] = jnp.where(sub == place, upper * lax.rsqrt(pivot), done[at])
        done[at] = jnp.where(sub == place + 1, lower * lax.rsqrt(second), done[at])
        upper = upper * inverse
        lower = lower * (1.0 / second)
        for t in range(at, tiles):
            one, two = near[t - at], far[t - at]
            take = one * upper + (two - one * ratio) * lower
            rows[t] = rows[t] - (jnp.where(sub > place + 1, take, 0.0) if t == at else take)
    return pltpu.roll(jnp.concatenate(done), half, 1)


def partials_of(narrow, recv, block, refs):
    ring = recv.shape[0]
    rank = narrow.shape[0]
    square = dot(narrow, narrow, ((1,), (1,)))
    for ref in refs:
        ref[:, ring * block:] = jnp.zeros((rank, LANES), jnp.float32)
        ref[:, ring * block:ring * block + rank] = square
    for j in range(ring):
        part = dot(narrow, recv[j, :block], ((1,), (1,)))
        for ref in refs:
            ref[:, j * block:(j + 1) * block] = part


def totals_of(spot, got, gram, block, ring):
    rank = got.shape[1]
    total = got[0]
    for copy in range(1, got.shape[0]):
        total = total + got[copy]
    wide = total[:, :ring * block]
    gram[...] = total[:, ring * block:]

    @pl.when(spot[1] == 0)
    def _():
        gram[:, :rank] = dot(wide, wide, ((1,), (1,)))

    return wide


def times_matrix(wide, recv, block):
    return sum(dot(wide[:, j * block:(j + 1) * block], recv[j, :block], ((1,), (0,))) for j in range(recv.shape[0]))


def first_kernel(block, spot, recv, start_query, start_output, sent, narrow, gram):
    @pl.when(spot[1] == 0)
    def _():
        narrow[...] = start_query[...]

    @pl.when(spot[1] == 1)
    def _():
        narrow[...] = times_matrix(start_output[...], recv, block)

    partials_of(narrow[...], recv, block, [sent.at[peer] for peer in range(sent.shape[0])])


def middle_kernel(block, spot, recv, got, sent, narrow, gram, stage, sems):
    ring = recv.shape[0]
    rank = got.shape[1]
    wide = totals_of(spot, got, gram, block, ring)
    plain = times_matrix(wide, recv, block)
    onward = [dot(plain, recv[j, :block], ((1,), (1,))) for j in range(ring)]
    inverse = invert_lower(gram[...])[:, :rank]
    value = dot(inverse, plain, ((1,), (0,)))
    narrow[...] = value
    half = ring // 2 * block
    parts = slice(0, half), slice(half, stage.shape[1])
    copies = [
        pltpu.make_async_copy(stage.at[:, part], sent.at[peer, :, part], sems.at[n, peer])
        for n, part in enumerate(parts) for peer in range(sent.shape[0])
    ]
    peers = sent.shape[0]
    stage[:, parts[0]] = dot(inverse, jnp.concatenate(onward[:ring // 2], axis=1), ((1,), (0,)))
    for copy in copies[:peers]:
        copy.start()
    stage[:, half:ring * block] = dot(inverse, jnp.concatenate(onward[ring // 2:], axis=1), ((1,), (0,)))
    stage[:, ring * block:] = jnp.zeros((rank, LANES), jnp.float32)
    stage[:, ring * block:ring * block + rank] = dot(value, value, ((1,), (1,)))
    for copy in copies[peers:]:
        copy.start()
    for copy in copies:
        copy.wait()


def last_kernel(block, spot, recv, got, narrow, factors, gram):
    ring = recv.shape[0]
    rank = got.shape[1]
    wide = totals_of(spot, got, gram, block, ring)
    plain = jnp.where(spot[1] == 0, times_matrix(wide, recv, block), narrow[...])
    inverse = invert_lower(gram[...])[:, :rank]
    factors[:, :ring * block] = dot(inverse, wide, ((1,), (0,)))
    factors[:, ring * block:] = dot(inverse, plain, ((1,), (0,)))


def final_kernel(
    block, shards, spot, kept_mine, kept_other, mine, other, grad_query, error_query, grad_output, error_output,
    moment_query, moment_output, new_error_query, new_error_output, new_moment_query, new_moment_output,
    new_weight_query, new_weight_output, error_q, error_o, weight_q, weight_o, kept, sems,
):
    height, width = error_query.shape
    rows = moment_query.shape[0]
    scale = 1.0 / shards
    ring = height // block
    index = spot[0]

    def copies(j):
        down = pl.ds(j * block, block)
        return (
            pltpu.make_async_copy(error_q.at[down], new_error_query.at[down], sems.at[0, j]),
            pltpu.make_async_copy(error_o.at[:, down], new_error_output.at[:, down], sems.at[1, j]),
            pltpu.make_async_copy(weight_q.at[down], new_weight_query.at[down], sems.at[2, j]),
            pltpu.make_async_copy(weight_o.at[:, down], new_weight_output.at[:, down], sems.at[3, j]),
        )

    loads = [
        pltpu.make_async_copy(source, kept.at[n], sems.at[4, n]) for n, source in enumerate((kept_mine, kept_other))
    ]
    for load in loads:
        load.start()

    def body(query, output, kept_query, kept_output):
        right = query[:, height:] * scale
        left = output[:, height:] * scale
        for j in range(ring):
            down = slice(j * block, (j + 1) * block)
            approx = dot(query[:, down], right, ((0,), (0,)))
            error_q[down] = grad_query[down].astype(jnp.float32) + error_query[down] - approx
            weight_q[down] = -0.01 * approx
            approx = dot(left, output[:, down], ((0,), (0,)))
            error_o[:, down] = grad_output[:, down].astype(jnp.float32) + error_output[:, down] - approx
            weight_o[:, down] = -0.01 * approx
            for copy in copies(j)[:2]:
                copy.start()
        for load in loads:
            load.wait()
        for j in range(ring):
            down = slice(j * block, (j + 1) * block)
            weight_q[down] = kept[kept_query, down] + weight_q[down]
            weight_o[:, down] = kept[kept_output, down] + weight_o[:, down]
            for copy in copies(j)[2:]:
                copy.start()
        along = index * rows
        base = pl.multiple_of(along // LANES * LANES, LANES)
        picked = pltpu.roll(query[:, pl.ds(base, LANES)], (LANES - along % LANES) % LANES, 1)
        new_moment_query[...] = 0.9 * moment_query[...] + dot(picked, right, ((0,), (0,)))[:rows]
        picked = pltpu.roll(output[:, pl.ds(base, LANES)], (LANES - along % LANES) % LANES, 1)
        new_moment_output[...] = 0.9 * moment_output[...] + dot(picked, left, ((0,), (0,)))[:rows]

    @pl.when(spot[1] == 0)
    def _():
        body(mine, other, 0, 1)

    @pl.when(spot[1] == 1)
    def _():
        body(other, mine, 1, 0)

    for j in range(ring):
        for copy in copies(j):
            copy.wait()


def prelude_kernel(ring, per, slot, vec, spot, *refs):
    far, total, near, (line, sems) = refs[:11], refs[11], refs[12:23], refs[23:]
    moves = [pltpu.make_async_copy(*pair, sems.at[n]) for n, pair in enumerate(zip(far, near))]
    grad_q, error_q, grad_o, error_o, grad_vector, weight_query, moment_query, weight_output, moment_output = near[:9]
    weight_vector, moment_vector = near[9:]
    height, width = grad_q.shape
    block = height // ring
    tall = block + slot
    rows = weight_query.shape[0]
    small = weight_vector.shape[1]
    index, which = spot[0], spot[1]

    @pl.when(which == 0)
    def _():
        moves[0].start()
        moves[1].start()

    @pl.when(which == 1)
    def _():
        moves[2].start()
        moves[3].start()

    for move in moves[4:]:
        move.start()
    for move in moves[4:]:
        move.wait()
    line[...] = jnp.zeros_like(line)
    line[0:1, :small] = weight_vector[...] - 0.009 * moment_vector[...]
    first = index * small
    spread = pltpu.roll(jnp.broadcast_to(line[0:1], (slot, LANES)), first % LANES, 1)
    sub = lax.broadcasted_iota(jnp.int32, (slot, LANES), 0)
    lane = lax.broadcasted_iota(jnp.int32, (slot, LANES), 1)
    for j in range(ring):
        after = LANES * (per * j + sub - per) + lane - first
        inside = (sub >= per) & (sub < 2 * per) & (after >= 0) & (after < small)
        total[j * tall + block:(j + 1) * tall] = jnp.where(inside, spread, 0.0)
        for n in range(per):
            r = per * j + n
            if r * LANES < vec:
                row = grad_vector[:, r * LANES:(r + 1) * LANES].astype(jnp.float32)
                total[j * tall + block + n:j * tall + block + n + 1] = row

    @pl.when(which == 0)
    def _():
        total[ring * tall:] = weight_query[...] - 0.009 * moment_query[...]
        moves[0].wait()
        moves[1].wait()
        for j in range(ring):
            down = slice(j * block, (j + 1) * block)
            total[j * tall:j * tall + block] = grad_q[down].astype(jnp.float32) + error_q[down]

    @pl.when(which == 1)
    def _():
        total[ring * tall:] = weight_output[...] - 0.009 * moment_output[...]
        moves[2].wait()
        moves[3].wait()
        for j in range(ring):
            down = slice(j * block, (j + 1) * block)
            total[j * tall:j * tall + block] = grad_o[:, down].astype(jnp.float32) + error_o[:, down]


def vector_kernel(block, per, shards, spot, recv, moment_vector, new_moment, new_weight, mean, kept):
    ring = recv.shape[0]
    small = moment_vector.shape[1]
    for j in range(ring):
        mean[per * j:per * (j + 1)] = recv[j, block:block + per] * (1.0 / shards)
        kept[per * j:per * (j + 1)] = recv[j, block + per:block + 2 * per]
    mean[per * ring:] = jnp.zeros((mean.shape[0] - per * ring, LANES), jnp.float32)
    lines = new_weight.shape[0]
    new_weight[...] = kept[:lines] - 0.01 * mean[:lines]
    first = spot[0] * small
    row, off = first // LANES, first % LANES
    shift = (LANES - off) % LANES
    one = pltpu.roll(jnp.broadcast_to(mean[pl.ds(row, 1)], (8, LANES)), shift, 1)
    two = pltpu.roll(jnp.broadcast_to(mean[pl.ds(row + 1, 1)], (8, LANES)), shift, 1)
    lane = lax.broadcasted_iota(jnp.int32, (8, LANES), 1)
    own = jnp.where(lane < LANES - off, one, two)
    new_moment[...] = 0.9 * moment_vector[...] + own[0:1, :small]


def shape(*dims):
    return jax.ShapeDtypeStruct(dims, jnp.float32)


def run(kernel, given, out_shape, scratch, out_specs=None, outside=0, **options):
    whole = pl.BlockSpec(memory_space=pltpu.VMEM)
    left = [pl.BlockSpec(memory_space=pltpu.HBM)] * outside
    specs = [pl.BlockSpec(memory_space=pltpu.SMEM)] + left + [whole] * (len(given) - 1 - outside)
    if out_specs is None:
        out_specs = jax.tree.map(lambda _: whole, out_shape)
    return pl.pallas_call(
        kernel, out_shape=out_shape, in_specs=specs, out_specs=out_specs, scratch_shapes=scratch,
        compiler_params=pltpu.CompilerParams(vmem_limit_bytes=40 * 2**20), **options,
    )(*given)


def local(
    grad_query,
    error_query,
    grad_output,
    error_output,
    start_query,
    start_output,
    weight_query,
    weight_output,
    moment_query,
    moment_output,
    grad_vector,
    moment_vector,
    weight_vector,
):
    shards = lax.axis_size("shard")
    tensors = lax.axis_size("tensor")
    index = lax.axis_index("shard")
    ring = ring_size(shards)
    first, second = groups(ring)
    asks = (index % 2) == 1
    width = start_query.shape[0]
    height = start_output.shape[0]
    rank = start_query.shape[1]
    block = height // ring
    rows = height // shards
    vec = grad_vector.shape[1]
    small = vec // shards
    lines = vec // LANES
    per = -(-lines // ring)
    slot = -(-2 * per // 8) * 8
    tall = block + slot
    assert width == LANES and rows * shards == height and small * shards == vec and lines * LANES == vec

    spot = jnp.stack([index, 1 - index % 2]).astype(jnp.int32)
    given = (
        grad_query[0], error_query[0], grad_output[0], error_output[0], grad_vector, weight_query, moment_query,
        weight_output.T, moment_output.T, weight_vector[None], moment_vector[None],
    )
    given = [pltpu.with_memory_space_constraint(value, pltpu.HBM) for value in given]

    def prelude(spot):
        return run(
            functools.partial(prelude_kernel, ring, per, slot, vec), (spot, *given), shape(ring * tall + rows, LANES),
            [
                *(pltpu.VMEM(value.shape, value.dtype) for value in given),
                pltpu.VMEM((8, LANES), jnp.float32), pltpu.SemaphoreType.DMA((len(given),)),
            ],
            outside=len(given),
        )

    got = swap_cores(prelude(jnp.stack([index, index % 2]).astype(jnp.int32)), shards)
    mine = prelude(spot)
    summed = (mine[:ring * tall] + got[:ring * tall]).reshape(ring, tall, LANES)
    own_kept, got_kept = mine[ring * tall:], got[ring * tall:]
    pair_kept = jnp.where(asks, jnp.concatenate([got_kept, own_kept]), jnp.concatenate([own_kept, got_kept]))

    part = exchange(summed, first).sum(0)
    every = share(jnp.concatenate([part, pair_kept]), second, ring)
    whole = every[:, :tall].sum(0)
    square = jnp.where(asks, whole[:block], whole[:block].T)
    kept_rows = every[:, tall:].reshape(block, LANES)
    every = share(jnp.concatenate([square, whole[block:], kept_rows]), first, ring)

    gram = pltpu.VMEM((rank, LANES), jnp.float32)
    partials = shape(tensors, rank, height + LANES)

    def gathered(value):
        return lax.all_to_all(value, "tensor", 0, 0, tiled=True)

    stage = [pltpu.VMEM((rank, height + LANES), jnp.float32), pltpu.SemaphoreType.DMA((2, tensors))]
    outside, within = pl.BlockSpec(memory_space=pl.ANY), pl.BlockSpec(memory_space=pltpu.VMEM)
    sent, narrow = run(
        functools.partial(first_kernel, block), (spot, every, start_query.T, start_output.T),
        (partials, shape(rank, width)), [gram],
    )
    for turn in range(ROUNDS - 1):
        sent, narrow = run(
            functools.partial(middle_kernel, block), (spot, every, gathered(sent)), (partials, shape(rank, width)),
            [gram, *stage], (outside, within),
        )

    sent, every = lax.optimization_barrier((sent, every))
    kept_all = every[:, tall:].reshape(ring, ring, 2 * rows, LANES)
    kept_turned = kept_all.transpose(1, 0, 2, 3).reshape(ring, block, LANES).transpose(0, 2, 1)
    kept_all = jnp.where(asks, kept_all.reshape(ring, block, LANES), kept_turned).reshape(height, LANES)
    kept_other = swap_cores(kept_all, shards)
    new_moment_vector, new_weight_vector = run(
        functools.partial(vector_kernel, block, per, shards), (spot, every, moment_vector[None]),
        (shape(1, small), shape(lines, LANES)),
        [pltpu.VMEM((per * ring + 8, LANES), jnp.float32), pltpu.VMEM((per * ring, LANES), jnp.float32)],
    )
    got, new_moment_vector, new_weight_vector = lax.optimization_barrier(
        (gathered(sent), new_moment_vector, new_weight_vector)
    )
    mine = run(functools.partial(last_kernel, block), (spot, every, got, narrow), shape(rank, height + width), [gram])
    other = swap_cores(mine, shards)
    big = [pltpu.VMEM((height, width), jnp.float32), pltpu.VMEM((width, height), jnp.float32)]
    (
        new_error_query, new_error_output, new_moment_query, new_moment_output, new_weight_query, new_weight_output,
    ) = run(
        functools.partial(final_kernel, block, shards),
        (
            spot, kept_all, kept_other, mine, other, grad_query[0], error_query[0], grad_output[0], error_output[0],
            moment_query, moment_output.T,
        ),
        (shape(height, width), shape(width, height), shape(rows, width), shape(rows, width), shape(height, width), shape(width, height)),
        [big[0], big[1], big[0], big[1], pltpu.VMEM((2, height, width), jnp.float32), pltpu.SemaphoreType.DMA((5, ring))],
        (outside, outside, within, within, outside, outside), 2,
    )
    new_error_query = new_error_query[None]
    new_error_output = new_error_output[None]
    new_moment_output = new_moment_output.T
    return (
        new_error_query,
        new_error_output,
        new_moment_query,
        new_moment_output,
        new_weight_query,
        new_weight_output,
        new_moment_vector[0],
        new_weight_vector.reshape(vec),
    )


def solution(mesh):
    in_specs = (
        P("shard", None, "tensor"),
        P("shard", None, "tensor"),
        P("shard", "tensor", None),
        P("shard", "tensor", None),
        P("tensor", None),
        P(),
        P("shard", "tensor"),
        P("tensor", "shard"),
        P("shard", "tensor"),
        P("tensor", "shard"),
        P("shard", None),
        P("shard"),
        P("shard"),
    )
    out_specs = (
        P("shard", None, "tensor"),
        P("shard", "tensor", None),
        P("shard", "tensor"),
        P("tensor", "shard"),
        P(None, "tensor"),
        P("tensor", None),
        P("shard"),
        P(),
    )
    return jax.shard_map(local, mesh=mesh, in_specs=in_specs, out_specs=out_specs, check_vma=False)
```

```python
import functools

import jax
import jax.numpy as jnp
from jax import lax
from jax.experimental import pallas as pl
from jax.experimental.pallas import tpu as pltpu
from jax.sharding import PartitionSpec as P

ROUNDS = 2
LANES = 128

highest = lax.Precision.HIGHEST


def dot(left, right, dims):
    return lax.dot_general(left, right, (dims, ((), ())), precision=highest, preferred_element_type=jnp.float32)


def ring_size(shards):
    ring = int(round((shards // 2) ** 0.5))
    assert 2 * ring * ring == shards
    return ring


def groups(ring):
    along_y = [[[(2 * (ring * y + z)) + c for y in range(ring)] for z in range(ring)] for c in range(2)]
    along_z = [[[(2 * (ring * y + z)) + c for z in range(ring)] for y in range(ring)] for c in range(2)]
    return along_z[0] + along_y[1], along_y[0] + along_z[1]


def swap_cores(value, shards):
    return lax.ppermute(value, "shard", [(s, s ^ 1) for s in range(shards)])


def exchange(value, group):
    return lax.all_to_all(value, "shard", 0, 0, axis_index_groups=group, tiled=True)


def share(value, group, size):
    return exchange(jnp.broadcast_to(value[None], (size, *value.shape)), group)


def invert_lower(gram):
    rank = gram.shape[0]
    tiles = rank // 8
    half = LANES // 2
    lane = lax.broadcasted_iota(jnp.int32, (8, LANES), 1)
    sub = lax.broadcasted_iota(jnp.int32, (8, LANES), 0)
    rows = [
        jnp.where(lane < rank, gram[8 * t:8 * t + 8], jnp.where(lane == sub + (8 * t + half), 1.0, 0.0))
        for t in range(tiles)
    ]
    done = [jnp.zeros((8, LANES), jnp.float32) for _ in range(tiles)]
    wide = (8, LANES)
    for k in range(0, rank, 2):
        at, place = k // 8, k % 8
        near = [jnp.broadcast_to(rows[t][:, k:k + 1], wide) for t in range(at, tiles)]
        far = [jnp.broadcast_to(rows[t][:, k + 1:k + 2], wide) for t in range(at, tiles)]
        upper = jnp.broadcast_to(rows[at][place:place + 1], wide)
        lower = jnp.broadcast_to(rows[at][place + 1:place + 2], wide)
        pivot = jnp.broadcast_to(near[0][place:place + 1], wide)
        below = jnp.broadcast_to(near[0][place + 1:place + 2], wide)
        corner = jnp.broadcast_to(far[0][place + 1:place + 2], wide)
        inverse = 1.0 / pivot
        ratio = below * inverse
        second = corner - below * ratio
        lower = lower - ratio * upper
        done[at] = jnp.where(sub == place, upper * lax.rsqrt(pivot), done[at])
        done[at] = jnp.where(sub == place + 1, lower * lax.rsqrt(second), done[at])
        upper = upper * inverse
        lower = lower * (1.0 / second)
        for t in range(at, tiles):
            one, two = near[t - at], far[t - at]
            take = one * upper + (two - one * ratio) * lower
            rows[t] = rows[t] - (jnp.where(sub > place + 1, take, 0.0) if t == at else take)
    return pltpu.roll(jnp.concatenate(done), half, 1)


def partials_of(narrow, recv, block, refs):
    ring = recv.shape[0]
    rank = narrow.shape[0]
    square = dot(narrow, narrow, ((1,), (1,)))
    for ref in refs:
        ref[:, ring * block:] = jnp.zeros((rank, LANES), jnp.float32)
        ref[:, ring * block:ring * block + rank] = square
    for j in range(ring):
        part = dot(recv[j, :block], narrow, ((1,), (1,))).T
        for ref in refs:
            ref[:, j * block:(j + 1) * block] = part


def totals_of(spot, got, gram, block, ring):
    rank = got.shape[1]
    total = got[0]
    for copy in range(1, got.shape[0]):
        total = total + got[copy]
    wide = total[:, :ring * block]
    gram[...] = total[:, ring * block:]

    @pl.when(spot[1] == 0)
    def _():
        gram[:, :rank] = dot(wide, wide, ((1,), (1,)))

    return wide


def times_matrix(wide, recv, block):
    return dot(wide, recv[:, :block].reshape(-1, block), ((1,), (0,)))


def first_kernel(block, spot, recv, start_query, start_output, sent, narrow, gram):
    @pl.when(spot[1] == 0)
    def _():
        narrow[...] = start_query[...]

    @pl.when(spot[1] == 1)
    def _():
        narrow[...] = times_matrix(start_output[...], recv, block)

    partials_of(narrow[...], recv, block, [sent.at[peer] for peer in range(sent.shape[0])])


def middle_kernel(block, spot, recv, got, sent, narrow, gram, stage, sems):
    ring = recv.shape[0]
    rank = got.shape[1]
    wide = totals_of(spot, got, gram, block, ring)
    plain = times_matrix(wide, recv, block)
    onward = [dot(plain, recv[j, :block], ((1,), (1,))) for j in range(ring)]
    inverse = invert_lower(gram[...])[:, :rank]
    value = dot(inverse, plain, ((1,), (0,)))
    narrow[...] = value
    half = ring // 2 * block
    parts = slice(0, half), slice(half, stage.shape[1])
    copies = [
        pltpu.make_async_copy(stage.at[:, part], sent.at[peer, :, part], sems.at[n, peer])
        for n, part in enumerate(parts) for peer in range(sent.shape[0])
    ]
    peers = sent.shape[0]
    stage[:, parts[0]] = dot(inverse, jnp.concatenate(onward[:ring // 2], axis=1), ((1,), (0,)))
    for copy in copies[:peers]:
        copy.start()
    stage[:, half:ring * block] = dot(inverse, jnp.concatenate(onward[ring // 2:], axis=1), ((1,), (0,)))
    stage[:, ring * block:] = jnp.zeros((rank, LANES), jnp.float32)
    stage[:, ring * block:ring * block + rank] = dot(value, value, ((1,), (1,)))
    for copy in copies[peers:]:
        copy.start()
    for copy in copies:
        copy.wait()


def last_kernel(block, spot, recv, got, narrow, factors, gram):
    ring = recv.shape[0]
    rank = got.shape[1]
    wide = totals_of(spot, got, gram, block, ring)
    plain = jnp.where(spot[1] == 0, times_matrix(wide, recv, block), narrow[...])
    inverse = invert_lower(gram[...])[:, :rank]
    factors[:, :ring * block] = dot(inverse, wide, ((1,), (0,)))
    factors[:, ring * block:] = dot(inverse, plain, ((1,), (0,)))


def final_kernel(block, shards, earlier, spot, *refs):
    refs = refs[earlier:]
    old, factors, grad_query, error_query, grad_output, error_output, moment_query, moment_output = refs[:8]
    (new_error_query, new_error_output, new_moment_query, new_moment_output, new_weight_query, new_weight_output) = refs[8:14]
    error_q, error_o, weight_q, weight_o, moment, kept, sems = refs[14:]
    height, width = error_query.shape
    rows = moment_query.shape[0]
    ring = height // block
    scale = 1.0 / shards
    load = pltpu.make_async_copy(old, kept, sems.at[2, 0])
    load.start()
    along = spot[0] * rows
    base = pl.multiple_of(along // LANES * LANES, LANES)
    picked = pltpu.roll(factors[:, pl.ds(base, LANES)], (LANES - along % LANES) % LANES, 1)
    narrow = factors[:, height:] * scale
    change = dot(picked, narrow, ((0,), (0,)))[:rows]

    def parts(j):
        down = pl.ds(j * block, block)
        return down, slice(j * block, (j + 1) * block)

    @pl.when(spot[1] == 0)
    def _():
        moment[...] = 0.9 * moment_query[...] + change
        copies = [pltpu.make_async_copy(moment, new_moment_query, sems.at[2, 1])]
        copies[0].start()
        for j in range(ring):
            at, down = parts(j)
            approx = dot(factors[:, down], narrow, ((0,), (0,)))
            error_q[down] = grad_query[down].astype(jnp.float32) + error_query[down] - approx
            weight_q[down] = -0.01 * approx
            copies.append(pltpu.make_async_copy(error_q.at[at], new_error_query.at[at], sems.at[0, j]))
            copies[-1].start()
        load.wait()
        for j in range(ring):
            at, down = parts(j)
            weight_q[down] = kept[down] + weight_q[down]
            copies.append(pltpu.make_async_copy(weight_q.at[at], new_weight_query.at[at], sems.at[1, j]))
            copies[-1].start()
        for copy in copies:
            copy.wait()

    @pl.when(spot[1] == 1)
    def _():
        moment[...] = 0.9 * moment_output[...] + change
        copies = [pltpu.make_async_copy(moment, new_moment_output, sems.at[2, 1])]
        copies[0].start()
        for j in range(ring):
            at, down = parts(j)
            approx = dot(narrow, factors[:, down], ((0,), (0,)))
            error_o[:, down] = grad_output[:, down].astype(jnp.float32) + error_output[:, down] - approx
            weight_o[:, down] = -0.01 * approx
            copies.append(pltpu.make_async_copy(error_o.at[:, at], new_error_output.at[:, at], sems.at[0, j]))
            copies[-1].start()
        load.wait()
        for j in range(ring):
            at, down = parts(j)
            weight_o[:, down] = kept[down] + weight_o[:, down]
            copies.append(pltpu.make_async_copy(weight_o.at[:, at], new_weight_output.at[:, at], sems.at[1, j]))
            copies[-1].start()
        for copy in copies:
            copy.wait()


def prelude_kernel(ring, per, slot, vec, spot, *refs):
    far, total, near, (line, sems) = refs[:11], refs[11], refs[12:23], refs[23:]
    moves = [pltpu.make_async_copy(*pair, sems.at[n]) for n, pair in enumerate(zip(far, near))]
    grad_q, error_q, grad_o, error_o, grad_vector, weight_query, moment_query, weight_output, moment_output = near[:9]
    weight_vector, moment_vector = near[9:]
    height, width = grad_q.shape
    block = height // ring
    tall = block + slot
    rows = weight_query.shape[0]
    small = weight_vector.shape[1]
    index, which = spot[0], spot[1]

    @pl.when(which == 0)
    def _():
        moves[0].start()
        moves[1].start()

    @pl.when(which == 1)
    def _():
        moves[2].start()
        moves[3].start()

    for move in moves[4:]:
        move.start()
    for move in moves[4:]:
        move.wait()
    line[...] = jnp.zeros_like(line)
    line[0:1, :small] = weight_vector[...] - 0.009 * moment_vector[...]
    first = index * small
    spread = pltpu.roll(jnp.broadcast_to(line[0:1], (slot, LANES)), first % LANES, 1)
    sub = lax.broadcasted_iota(jnp.int32, (slot, LANES), 0)
    lane = lax.broadcasted_iota(jnp.int32, (slot, LANES), 1)
    for j in range(ring):
        after = LANES * (per * j + sub - per) + lane - first
        inside = (sub >= per) & (sub < 2 * per) & (after >= 0) & (after < small)
        total[j * tall + block:(j + 1) * tall] = jnp.where(inside, spread, 0.0)
        for n in range(per):
            r = per * j + n
            if r * LANES < vec:
                row = grad_vector[:, r * LANES:(r + 1) * LANES].astype(jnp.float32)
                total[j * tall + block + n:j * tall + block + n + 1] = row

    @pl.when(which == 0)
    def _():
        total[ring * tall:] = weight_query[...] - 0.009 * moment_query[...]
        moves[0].wait()
        moves[1].wait()
        for j in range(ring):
            down = slice(j * block, (j + 1) * block)
            total[j * tall:j * tall + block] = grad_q[down].astype(jnp.float32) + error_q[down]

    @pl.when(which == 1)
    def _():
        total[ring * tall:] = weight_output[...] - 0.009 * moment_output[...]
        moves[2].wait()
        moves[3].wait()
        for j in range(ring):
            down = slice(j * block, (j + 1) * block)
            total[j * tall:j * tall + block] = grad_o[:, down].astype(jnp.float32) + error_o[:, down]


def vector_kernel(block, per, shards, spot, recv, moment_vector, new_moment, new_weight, mean, kept):
    ring = recv.shape[0]
    small = moment_vector.shape[1]
    for j in range(ring):
        mean[per * j:per * (j + 1)] = recv[j, block:block + per] * (1.0 / shards)
        kept[per * j:per * (j + 1)] = recv[j, block + per:block + 2 * per]
    mean[per * ring:] = jnp.zeros((mean.shape[0] - per * ring, LANES), jnp.float32)
    lines = new_weight.shape[0]
    new_weight[...] = kept[:lines] - 0.01 * mean[:lines]
    first = spot[0] * small
    row, off = first // LANES, first % LANES
    shift = (LANES - off) % LANES
    one = pltpu.roll(jnp.broadcast_to(mean[pl.ds(row, 1)], (8, LANES)), shift, 1)
    two = pltpu.roll(jnp.broadcast_to(mean[pl.ds(row + 1, 1)], (8, LANES)), shift, 1)
    lane = lax.broadcasted_iota(jnp.int32, (8, LANES), 1)
    own = jnp.where(lane < LANES - off, one, two)
    new_moment[...] = 0.9 * moment_vector[...] + own[0:1, :small]


def shape(*dims):
    return jax.ShapeDtypeStruct(dims, jnp.float32)


def run(kernel, given, out_shape, scratch, out_specs=None, outside=0, **options):
    whole = pl.BlockSpec(memory_space=pltpu.VMEM)
    left = [pl.BlockSpec(memory_space=pltpu.HBM)] * outside
    specs = [pl.BlockSpec(memory_space=pltpu.SMEM)] + left + [whole] * (len(given) - 1 - outside)
    if out_specs is None:
        out_specs = jax.tree.map(lambda _: whole, out_shape)
    return pl.pallas_call(
        kernel, out_shape=out_shape, in_specs=specs, out_specs=out_specs, scratch_shapes=scratch,
        compiler_params=pltpu.CompilerParams(vmem_limit_bytes=40 * 2**20), **options,
    )(*given)


def local(
    grad_query,
    error_query,
    grad_output,
    error_output,
    start_query,
    start_output,
    weight_query,
    weight_output,
    moment_query,
    moment_output,
    grad_vector,
    moment_vector,
    weight_vector,
):
    shards = lax.axis_size("shard")
    tensors = lax.axis_size("tensor")
    index = lax.axis_index("shard")
    ring = ring_size(shards)
    first, second = groups(ring)
    asks = (index % 2) == 1
    width = start_query.shape[0]
    height = start_output.shape[0]
    rank = start_query.shape[1]
    block = height // ring
    rows = height // shards
    vec = grad_vector.shape[1]
    small = vec // shards
    lines = vec // LANES
    per = -(-lines // ring)
    slot = -(-2 * per // 8) * 8
    tall = block + slot
    assert width == LANES and rows * shards == height and small * shards == vec and lines * LANES == vec

    spot = jnp.stack([index, 1 - index % 2]).astype(jnp.int32)
    given = (
        grad_query[0], error_query[0], grad_output[0], error_output[0], grad_vector, weight_query, moment_query,
        weight_output.T, moment_output.T, weight_vector[None], moment_vector[None],
    )
    given = [pltpu.with_memory_space_constraint(value, pltpu.HBM) for value in given]

    def prelude(spot):
        return run(
            functools.partial(prelude_kernel, ring, per, slot, vec), (spot, *given), shape(ring * tall + rows, LANES),
            [
                *(pltpu.VMEM(value.shape, value.dtype) for value in given),
                pltpu.VMEM((8, LANES), jnp.float32), pltpu.SemaphoreType.DMA((len(given),)),
            ],
            outside=len(given),
        )

    swapped = jnp.stack([index, index % 2]).astype(jnp.int32)
    got = swap_cores(prelude(swapped), shards)
    mine = prelude(spot)
    summed = (mine[:ring * tall] + got[:ring * tall]).reshape(ring, tall, LANES)
    own_kept, got_kept = mine[ring * tall:], got[ring * tall:]
    pair_kept = jnp.where(asks, jnp.concatenate([got_kept, own_kept]), jnp.concatenate([own_kept, got_kept]))

    part = exchange(summed, first).sum(0)
    every = share(jnp.concatenate([part, pair_kept]), second, ring)
    whole = every[:, :tall].sum(0)
    square = jnp.where(asks, whole[:block], whole[:block].T)
    kept_rows = every[:, tall:].reshape(block, LANES)
    every = share(jnp.concatenate([square, whole[block:], kept_rows]), first, ring)

    gram = pltpu.VMEM((rank, LANES), jnp.float32)
    partials = shape(tensors, rank, height + LANES)

    def gathered(value):
        return lax.all_to_all(value, "tensor", 0, 0, tiled=True)

    stage = [pltpu.VMEM((rank, height + LANES), jnp.float32), pltpu.SemaphoreType.DMA((2, tensors))]
    outside, within = pl.BlockSpec(memory_space=pl.ANY), pl.BlockSpec(memory_space=pltpu.VMEM)
    sent, narrow = run(
        functools.partial(first_kernel, block), (spot, every, start_query.T, start_output.T),
        (partials, shape(rank, width)), [gram],
    )
    for turn in range(ROUNDS - 1):
        sent, narrow = run(
            functools.partial(middle_kernel, block), (spot, every, gathered(sent)), (partials, shape(rank, width)),
            [gram, *stage], (outside, within),
        )

    sent, every = lax.optimization_barrier((sent, every))
    kept_all = every[:, tall:].reshape(ring, ring, 2 * rows, LANES)
    kept_turned = kept_all.transpose(1, 0, 2, 3).reshape(ring, block, LANES).transpose(0, 2, 1)
    kept_all = jnp.where(asks, kept_all.reshape(ring, block, LANES), kept_turned).reshape(height, LANES)
    kept_other = swap_cores(kept_all, shards)
    new_moment_vector, new_weight_vector = run(
        functools.partial(vector_kernel, block, per, shards), (spot, every, moment_vector[None]),
        (shape(1, small), shape(lines, LANES)),
        [pltpu.VMEM((per * ring + 8, LANES), jnp.float32), pltpu.VMEM((per * ring, LANES), jnp.float32)],
    )
    got, new_moment_vector, new_weight_vector = lax.optimization_barrier(
        (gathered(sent), new_moment_vector, new_weight_vector)
    )
    mine = run(functools.partial(last_kernel, block), (spot, every, got, narrow), shape(rank, height + width), [gram])
    other = swap_cores(mine, shards)
    big = [pltpu.VMEM((height, width), jnp.float32), pltpu.VMEM((width, height), jnp.float32)]
    ends = (shape(height, width), shape(width, height), shape(rows, width), shape(rows, width), shape(height, width), shape(width, height))
    local_ones = (grad_query[0], error_query[0], grad_output[0], error_output[0], moment_query, moment_output.T)

    def final(spot, before, kept, factors):
        return run(
            functools.partial(final_kernel, block, shards, len(before)), (spot, *before, kept, factors, *local_ones), ends,
            [*big, *big, pltpu.VMEM((rows, width), jnp.float32), big[0], pltpu.SemaphoreType.DMA((3, ring))],
            (outside,) * 6, len(before) + 1, input_output_aliases={n + 1: n for n in range(len(before))},
        )

    ends_of_mine = final(spot, (), kept_all, mine)
    (
        new_error_query, new_error_output, new_moment_query, new_moment_output, new_weight_query, new_weight_output,
    ) = final(swapped, ends_of_mine, kept_other, other)
    new_error_query = new_error_query[None]
    new_error_output = new_error_output[None]
    new_moment_output = new_moment_output.T
    return (
        new_error_query,
        new_error_output,
        new_moment_query,
        new_moment_output,
        new_weight_query,
        new_weight_output,
        new_moment_vector[0],
        new_weight_vector.reshape(vec),
    )


def solution(mesh):
    in_specs = (
        P("shard", None, "tensor"),
        P("shard", None, "tensor"),
        P("shard", "tensor", None),
        P("shard", "tensor", None),
        P("tensor", None),
        P(),
        P("shard", "tensor"),
        P("tensor", "shard"),
        P("shard", "tensor"),
        P("tensor", "shard"),
        P("shard", None),
        P("shard"),
        P("shard"),
    )
    out_specs = (
        P("shard", None, "tensor"),
        P("shard", "tensor", None),
        P("shard", "tensor"),
        P("tensor", "shard"),
        P(None, "tensor"),
        P("tensor", None),
        P("shard"),
        P(),
    )
    return jax.shard_map(local, mesh=mesh, in_specs=in_specs, out_specs=out_specs, check_vma=False)
```

```python
import functools

import jax
import jax.numpy as jnp
from jax import lax
from jax.experimental import pallas as pl
from jax.experimental.pallas import tpu as pltpu
from jax.sharding import PartitionSpec as P

ROUNDS = 2
LANES = 128

highest = lax.Precision.HIGHEST


def dot(left, right, dims):
    return lax.dot_general(left, right, (dims, ((), ())), precision=highest, preferred_element_type=jnp.float32)


def ring_size(shards):
    ring = int(round((shards // 2) ** 0.5))
    assert 2 * ring * ring == shards
    return ring


def groups(ring):
    along_y = [[[(2 * (ring * y + z)) + c for y in range(ring)] for z in range(ring)] for c in range(2)]
    along_z = [[[(2 * (ring * y + z)) + c for z in range(ring)] for y in range(ring)] for c in range(2)]
    return along_z[0] + along_y[1], along_y[0] + along_z[1]


def swap_cores(value, shards):
    return lax.ppermute(value, "shard", [(s, s ^ 1) for s in range(shards)])


def exchange(value, group):
    return lax.all_to_all(value, "shard", 0, 0, axis_index_groups=group, tiled=True)


def share(value, group, size):
    return exchange(jnp.broadcast_to(value[None], (size, *value.shape)), group)


def invert_lower(gram):
    rank = gram.shape[0]
    tiles = rank // 8
    half = LANES // 2
    lane = lax.broadcasted_iota(jnp.int32, (8, LANES), 1)
    sub = lax.broadcasted_iota(jnp.int32, (8, LANES), 0)
    rows = [
        jnp.where(lane < rank, gram[8 * t:8 * t + 8], jnp.where(lane == sub + (8 * t + half), 1.0, 0.0))
        for t in range(tiles)
    ]
    done = [jnp.zeros((8, LANES), jnp.float32) for _ in range(tiles)]
    wide = (8, LANES)
    panel = 8
    for k in range(0, rank, panel):
        at, place = k // 8, k % 8
        below = range(at, tiles)
        columns = [[jnp.broadcast_to(rows[t][:, k + i:k + i + 1], wide) for t in below] for i in range(panel)]
        lines = [jnp.broadcast_to(rows[at][place + i:place + i + 1], wide) for i in range(panel)]
        for i in range(panel):
            pivot = jnp.broadcast_to(columns[i][0][place + i:place + i + 1], wide)
            inverse = 1.0 / pivot
            done[at] = jnp.where(sub == place + i, lines[i] * lax.rsqrt(pivot), done[at])
            scaled = lines[i] * inverse
            for l in range(i + 1, panel):
                entry = jnp.broadcast_to(columns[i][0][place + l:place + l + 1], wide)
                ratio = entry * inverse
                lines[l] = lines[l] - entry * scaled
                columns[l] = [one - two * ratio for one, two in zip(columns[l], columns[i])]
            lines[i] = scaled
        for t in below:
            take = sum(columns[i][t - at] * lines[i] for i in range(panel))
            rows[t] = rows[t] - (jnp.where(sub >= place + panel, take, 0.0) if t == at else take)
    return pltpu.roll(jnp.concatenate(done), half, 1)


def partials_of(narrow, recv, block, refs):
    ring = recv.shape[0]
    rank = narrow.shape[0]
    square = dot(narrow, narrow, ((1,), (1,)))
    for ref in refs:
        ref[:, ring * block:] = jnp.zeros((rank, LANES), jnp.float32)
        ref[:, ring * block:ring * block + rank] = square
    for j in range(ring):
        part = dot(recv[j, :block], narrow, ((1,), (1,))).T
        for ref in refs:
            ref[:, j * block:(j + 1) * block] = part


def totals_of(spot, got, gram, block, ring):
    rank = got.shape[1]
    total = got[0]
    for copy in range(1, got.shape[0]):
        total = total + got[copy]
    wide = total[:, :ring * block]
    gram[...] = total[:, ring * block:]

    @pl.when(spot[1] == 0)
    def _():
        gram[:, :rank] = dot(wide, wide, ((1,), (1,)))

    return wide


def times_matrix(wide, recv, block):
    return dot(wide, recv[:, :block].reshape(-1, block), ((1,), (0,)))


def first_kernel(block, spot, recv, start_query, start_output, sent, narrow, gram):
    @pl.when(spot[1] == 0)
    def _():
        narrow[...] = start_query[...]

    @pl.when(spot[1] == 1)
    def _():
        narrow[...] = times_matrix(start_output[...], recv, block)

    partials_of(narrow[...], recv, block, [sent.at[peer] for peer in range(sent.shape[0])])


def middle_kernel(block, spot, recv, got, sent, narrow, gram, stage, sems):
    ring = recv.shape[0]
    rank = got.shape[1]
    wide = totals_of(spot, got, gram, block, ring)
    plain = times_matrix(wide, recv, block)
    onward = [dot(plain, recv[j, :block], ((1,), (1,))) for j in range(ring)]
    inverse = invert_lower(gram[...])[:, :rank]
    value = dot(inverse, plain, ((1,), (0,)))
    narrow[...] = value
    half = ring // 2 * block
    parts = slice(0, half), slice(half, stage.shape[1])
    copies = [
        pltpu.make_async_copy(stage.at[:, part], sent.at[peer, :, part], sems.at[n, peer])
        for n, part in enumerate(parts) for peer in range(sent.shape[0])
    ]
    peers = sent.shape[0]
    stage[:, parts[0]] = dot(inverse, jnp.concatenate(onward[:ring // 2], axis=1), ((1,), (0,)))
    for copy in copies[:peers]:
        copy.start()
    stage[:, half:ring * block] = dot(inverse, jnp.concatenate(onward[ring // 2:], axis=1), ((1,), (0,)))
    stage[:, ring * block:] = jnp.zeros((rank, LANES), jnp.float32)
    stage[:, ring * block:ring * block + rank] = dot(value, value, ((1,), (1,)))
    for copy in copies[peers:]:
        copy.start()
    for copy in copies:
        copy.wait()


def last_kernel(block, spot, recv, got, narrow, factors, gram):
    ring = recv.shape[0]
    rank = got.shape[1]
    wide = totals_of(spot, got, gram, block, ring)
    plain = jnp.where(spot[1] == 0, times_matrix(wide, recv, block), narrow[...])
    inverse = invert_lower(gram[...])[:, :rank]
    factors[:, :ring * block] = dot(inverse, wide, ((1,), (0,)))
    factors[:, ring * block:] = dot(inverse, plain, ((1,), (0,)))


def final_kernel(block, shards, earlier, spot, *refs):
    refs = refs[earlier:]
    old, factors, grad_query, error_query, grad_output, error_output, moment_query, moment_output = refs[:8]
    (new_error_query, new_error_output, new_moment_query, new_moment_output, new_weight_query, new_weight_output) = refs[8:14]
    error_q, error_o, weight_q, weight_o, moment, kept, sems = refs[14:]
    height, width = error_query.shape
    rows = moment_query.shape[0]
    ring = height // block
    scale = 1.0 / shards
    load = pltpu.make_async_copy(old, kept, sems.at[2, 0])
    load.start()
    narrow = factors[:, height:] * scale

    def change():
        along = spot[0] * rows
        base = pl.multiple_of(along // LANES * LANES, LANES)
        picked = pltpu.roll(factors[:, pl.ds(base, LANES)], (LANES - along % LANES) % LANES, 1)
        return dot(picked, narrow, ((0,), (0,)))[:rows]

    def parts(j):
        down = pl.ds(j * block, block)
        return down, slice(j * block, (j + 1) * block)

    @pl.when(spot[1] == 0)
    def _():
        copies = []
        for j in range(ring):
            at, down = parts(j)
            approx = dot(factors[:, down], narrow, ((0,), (0,)))
            error_q[down] = grad_query[down].astype(jnp.float32) + error_query[down] - approx
            weight_q[down] = -0.01 * approx
            copies.append(pltpu.make_async_copy(error_q.at[at], new_error_query.at[at], sems.at[0, j]))
            copies[-1].start()
        moment[...] = 0.9 * moment_query[...] + change()
        copies.append(pltpu.make_async_copy(moment, new_moment_query, sems.at[2, 1]))
        copies[-1].start()
        load.wait()
        for j in range(ring):
            at, down = parts(j)
            weight_q[down] = kept[down] + weight_q[down]
            copies.append(pltpu.make_async_copy(weight_q.at[at], new_weight_query.at[at], sems.at[1, j]))
            copies[-1].start()
        for copy in copies:
            copy.wait()

    @pl.when(spot[1] == 1)
    def _():
        copies = []
        for j in range(ring):
            at, down = parts(j)
            approx = dot(narrow, factors[:, down], ((0,), (0,)))
            error_o[:, down] = grad_output[:, down].astype(jnp.float32) + error_output[:, down] - approx
            weight_o[:, down] = -0.01 * approx
            copies.append(pltpu.make_async_copy(error_o.at[:, at], new_error_output.at[:, at], sems.at[0, j]))
            copies[-1].start()
        moment[...] = 0.9 * moment_output[...] + change()
        copies.append(pltpu.make_async_copy(moment, new_moment_output, sems.at[2, 1]))
        copies[-1].start()
        load.wait()
        for j in range(ring):
            at, down = parts(j)
            weight_o[:, down] = kept[down] + weight_o[:, down]
            copies.append(pltpu.make_async_copy(weight_o.at[:, at], new_weight_output.at[:, at], sems.at[1, j]))
            copies[-1].start()
        for copy in copies:
            copy.wait()


def prelude_kernel(ring, per, slot, vec, spot, *refs):
    far, total, near, (line, sems) = refs[:11], refs[11], refs[12:23], refs[23:]
    moves = [pltpu.make_async_copy(*pair, sems.at[n]) for n, pair in enumerate(zip(far, near))]
    grad_q, error_q, grad_o, error_o, grad_vector, weight_query, moment_query, weight_output, moment_output = near[:9]
    weight_vector, moment_vector = near[9:]
    height, width = grad_q.shape
    block = height // ring
    tall = block + slot
    rows = weight_query.shape[0]
    small = weight_vector.shape[1]
    index, which = spot[0], spot[1]

    @pl.when(which == 0)
    def _():
        moves[0].start()
        moves[1].start()

    @pl.when(which == 1)
    def _():
        moves[2].start()
        moves[3].start()

    for move in moves[4:]:
        move.start()
    for move in moves[4:]:
        move.wait()
    line[...] = jnp.zeros_like(line)
    line[0:1, :small] = weight_vector[...] - 0.009 * moment_vector[...]
    first = index * small
    spread = pltpu.roll(jnp.broadcast_to(line[0:1], (slot, LANES)), first % LANES, 1)
    sub = lax.broadcasted_iota(jnp.int32, (slot, LANES), 0)
    lane = lax.broadcasted_iota(jnp.int32, (slot, LANES), 1)
    for j in range(ring):
        after = LANES * (per * j + sub - per) + lane - first
        inside = (sub >= per) & (sub < 2 * per) & (after >= 0) & (after < small)
        total[j * tall + block:(j + 1) * tall] = jnp.where(inside, spread, 0.0)
        for n in range(per):
            r = per * j + n
            if r * LANES < vec:
                row = grad_vector[:, r * LANES:(r + 1) * LANES].astype(jnp.float32)
                total[j * tall + block + n:j * tall + block + n + 1] = row

    @pl.when(which == 0)
    def _():
        total[ring * tall:] = weight_query[...] - 0.009 * moment_query[...]
        moves[0].wait()
        moves[1].wait()
        for j in range(ring):
            down = slice(j * block, (j + 1) * block)
            total[j * tall:j * tall + block] = grad_q[down].astype(jnp.float32) + error_q[down]

    @pl.when(which == 1)
    def _():
        total[ring * tall:] = weight_output[...] - 0.009 * moment_output[...]
        moves[2].wait()
        moves[3].wait()
        for j in range(ring):
            down = slice(j * block, (j + 1) * block)
            total[j * tall:j * tall + block] = grad_o[:, down].astype(jnp.float32) + error_o[:, down]


def vector_kernel(block, per, shards, spot, recv, moment_vector, new_moment, new_weight, mean, kept):
    ring = recv.shape[0]
    small = moment_vector.shape[1]
    for j in range(ring):
        mean[per * j:per * (j + 1)] = recv[j, block:block + per] * (1.0 / shards)
        kept[per * j:per * (j + 1)] = recv[j, block + per:block + 2 * per]
    mean[per * ring:] = jnp.zeros((mean.shape[0] - per * ring, LANES), jnp.float32)
    lines = new_weight.shape[0]
    new_weight[...] = kept[:lines] - 0.01 * mean[:lines]
    first = spot[0] * small
    row, off = first // LANES, first % LANES
    shift = (LANES - off) % LANES
    one = pltpu.roll(jnp.broadcast_to(mean[pl.ds(row, 1)], (8, LANES)), shift, 1)
    two = pltpu.roll(jnp.broadcast_to(mean[pl.ds(row + 1, 1)], (8, LANES)), shift, 1)
    lane = lax.broadcasted_iota(jnp.int32, (8, LANES), 1)
    own = jnp.where(lane < LANES - off, one, two)
    new_moment[...] = 0.9 * moment_vector[...] + own[0:1, :small]


def shape(*dims):
    return jax.ShapeDtypeStruct(dims, jnp.float32)


def run(kernel, given, out_shape, scratch, out_specs=None, outside=0, **options):
    whole = pl.BlockSpec(memory_space=pltpu.VMEM)
    left = [pl.BlockSpec(memory_space=pltpu.HBM)] * outside
    specs = [pl.BlockSpec(memory_space=pltpu.SMEM)] + left + [whole] * (len(given) - 1 - outside)
    if out_specs is None:
        out_specs = jax.tree.map(lambda _: whole, out_shape)
    return pl.pallas_call(
        kernel, out_shape=out_shape, in_specs=specs, out_specs=out_specs, scratch_shapes=scratch,
        compiler_params=pltpu.CompilerParams(vmem_limit_bytes=40 * 2**20), **options,
    )(*given)


def local(
    grad_query,
    error_query,
    grad_output,
    error_output,
    start_query,
    start_output,
    weight_query,
    weight_output,
    moment_query,
    moment_output,
    grad_vector,
    moment_vector,
    weight_vector,
):
    shards = lax.axis_size("shard")
    tensors = lax.axis_size("tensor")
    index = lax.axis_index("shard")
    ring = ring_size(shards)
    first, second = groups(ring)
    asks = (index % 2) == 1
    width = start_query.shape[0]
    height = start_output.shape[0]
    rank = start_query.shape[1]
    block = height // ring
    rows = height // shards
    vec = grad_vector.shape[1]
    small = vec // shards
    lines = vec // LANES
    per = -(-lines // ring)
    slot = -(-2 * per // 8) * 8
    tall = block + slot
    assert width == LANES and rows * shards == height and small * shards == vec and lines * LANES == vec

    spot = jnp.stack([index, 1 - index % 2]).astype(jnp.int32)
    given = (
        grad_query[0], error_query[0], grad_output[0], error_output[0], grad_vector, weight_query, moment_query,
        weight_output.T, moment_output.T, weight_vector[None], moment_vector[None],
    )
    given = [pltpu.with_memory_space_constraint(value, pltpu.HBM) for value in given]

    def prelude(spot):
        return run(
            functools.partial(prelude_kernel, ring, per, slot, vec), (spot, *given), shape(ring * tall + rows, LANES),
            [
                *(pltpu.VMEM(value.shape, value.dtype) for value in given),
                pltpu.VMEM((8, LANES), jnp.float32), pltpu.SemaphoreType.DMA((len(given),)),
            ],
            outside=len(given),
        )

    swapped = jnp.stack([index, index % 2]).astype(jnp.int32)
    got = swap_cores(prelude(swapped), shards)
    mine = prelude(spot)
    summed = (mine[:ring * tall] + got[:ring * tall]).reshape(ring, tall, LANES)
    summed = exchange(summed, first)
    summed, mine, got = lax.optimization_barrier((summed, mine, got))
    own_kept, got_kept = mine[ring * tall:], got[ring * tall:]
    pair_kept = jnp.where(asks, jnp.concatenate([got_kept, own_kept]), jnp.concatenate([own_kept, got_kept]))

    part = summed.sum(0)
    every = share(jnp.concatenate([part, pair_kept]), second, ring)
    whole = every[:, :tall].sum(0)
    square = jnp.where(asks, whole[:block], whole[:block].T)
    kept_rows = every[:, tall:].reshape(block, LANES)
    every = share(jnp.concatenate([square, whole[block:], kept_rows]), first, ring)

    gram = pltpu.VMEM((rank, LANES), jnp.float32)
    partials = shape(tensors, rank, height + LANES)

    def gathered(value):
        return lax.all_to_all(value, "tensor", 0, 0, tiled=True)

    stage = [pltpu.VMEM((rank, height + LANES), jnp.float32), pltpu.SemaphoreType.DMA((2, tensors))]
    outside, within = pl.BlockSpec(memory_space=pl.ANY), pl.BlockSpec(memory_space=pltpu.VMEM)
    sent, narrow = run(
        functools.partial(first_kernel, block), (spot, every, start_query.T, start_output.T),
        (partials, shape(rank, width)), [gram],
    )
    for turn in range(ROUNDS - 1):
        sent, narrow = run(
            functools.partial(middle_kernel, block), (spot, every, gathered(sent)), (partials, shape(rank, width)),
            [gram, *stage], (outside, within),
        )

    sent, every = lax.optimization_barrier((sent, every))
    kept_all = every[:, tall:].reshape(ring, ring, 2 * rows, LANES)
    kept_turned = kept_all.transpose(1, 0, 2, 3).reshape(ring, block, LANES).transpose(0, 2, 1)
    kept_all = jnp.where(asks, kept_all.reshape(ring, block, LANES), kept_turned).reshape(height, LANES)
    kept_other = swap_cores(kept_all, shards)
    new_moment_vector, new_weight_vector = run(
        functools.partial(vector_kernel, block, per, shards), (spot, every, moment_vector[None]),
        (shape(1, small), shape(lines, LANES)),
        [pltpu.VMEM((per * ring + 8, LANES), jnp.float32), pltpu.VMEM((per * ring, LANES), jnp.float32)],
    )
    got, new_moment_vector, new_weight_vector = lax.optimization_barrier(
        (gathered(sent), new_moment_vector, new_weight_vector)
    )
    mine = run(functools.partial(last_kernel, block), (spot, every, got, narrow), shape(rank, height + width), [gram])
    other = swap_cores(mine, shards)
    big = [pltpu.VMEM((height, width), jnp.float32), pltpu.VMEM((width, height), jnp.float32)]
    ends = (shape(height, width), shape(width, height), shape(rows, width), shape(rows, width), shape(height, width), shape(width, height))
    local_ones = (grad_query[0], error_query[0], grad_output[0], error_output[0], moment_query, moment_output.T)

    def final(spot, before, kept, factors):
        return run(
            functools.partial(final_kernel, block, shards, len(before)), (spot, *before, kept, factors, *local_ones), ends,
            [*big, *big, pltpu.VMEM((rows, width), jnp.float32), big[0], pltpu.SemaphoreType.DMA((3, ring))],
            (outside,) * 6, len(before) + 1, input_output_aliases={n + 1: n for n in range(len(before))},
        )

    ends_of_mine = final(spot, (), kept_all, mine)
    (
        new_error_query, new_error_output, new_moment_query, new_moment_output, new_weight_query, new_weight_output,
    ) = final(swapped, ends_of_mine, kept_other, other)
    new_error_query = new_error_query[None]
    new_error_output = new_error_output[None]
    new_moment_output = new_moment_output.T
    return (
        new_error_query,
        new_error_output,
        new_moment_query,
        new_moment_output,
        new_weight_query,
        new_weight_output,
        new_moment_vector[0],
        new_weight_vector.reshape(vec),
    )


def solution(mesh):
    in_specs = (
        P("shard", None, "tensor"),
        P("shard", None, "tensor"),
        P("shard", "tensor", None),
        P("shard", "tensor", None),
        P("tensor", None),
        P(),
        P("shard", "tensor"),
        P("tensor", "shard"),
        P("shard", "tensor"),
        P("tensor", "shard"),
        P("shard", None),
        P("shard"),
        P("shard"),
    )
    out_specs = (
        P("shard", None, "tensor"),
        P("shard", "tensor", None),
        P("shard", "tensor"),
        P("tensor", "shard"),
        P(None, "tensor"),
        P("tensor", None),
        P("shard"),
        P(),
    )
    return jax.shard_map(local, mesh=mesh, in_specs=in_specs, out_specs=out_specs, check_vma=False)
```

```python
import functools

import jax
import jax.numpy as jnp
from jax import lax
from jax.experimental import pallas as pl
from jax.experimental.pallas import tpu as pltpu
from jax.sharding import PartitionSpec as P

ROUNDS = 2
LANES = 128

highest = lax.Precision.HIGHEST


def dot(left, right, dims):
    return lax.dot_general(left, right, (dims, ((), ())), precision=highest, preferred_element_type=jnp.float32)


def ring_size(shards):
    ring = int(round((shards // 2) ** 0.5))
    assert 2 * ring * ring == shards
    return ring


def groups(ring):
    along_y = [[[(2 * (ring * y + z)) + c for y in range(ring)] for z in range(ring)] for c in range(2)]
    along_z = [[[(2 * (ring * y + z)) + c for z in range(ring)] for y in range(ring)] for c in range(2)]
    return along_z[0] + along_y[1], along_y[0] + along_z[1]


def swap_cores(value, shards):
    return lax.ppermute(value, "shard", [(s, s ^ 1) for s in range(shards)])


def exchange(value, group):
    return lax.all_to_all(value, "shard", 0, 0, axis_index_groups=group, tiled=True)


def share(value, group, size):
    return exchange(jnp.broadcast_to(value[None], (size, *value.shape)), group)


def invert_lower(gram):
    rank = gram.shape[0]
    tiles = rank // 8
    half = LANES // 2
    lane = lax.broadcasted_iota(jnp.int32, (8, LANES), 1)
    sub = lax.broadcasted_iota(jnp.int32, (8, LANES), 0)
    rows = [
        jnp.where(lane < rank, gram[8 * t:8 * t + 8], jnp.where(lane == sub + (8 * t + half), 1.0, 0.0))
        for t in range(tiles)
    ]
    done = [jnp.zeros((8, LANES), jnp.float32) for _ in range(tiles)]
    wide = (8, LANES)
    panel = 8
    for k in range(0, rank, panel):
        at, place = k // 8, k % 8
        below = range(at, tiles)
        columns = [[jnp.broadcast_to(rows[t][:, k + i:k + i + 1], wide) for t in below] for i in range(panel)]
        lines = [jnp.broadcast_to(rows[at][place + i:place + i + 1], wide) for i in range(panel)]
        for i in range(panel):
            pivot = jnp.broadcast_to(columns[i][0][place + i:place + i + 1], wide)
            inverse = 1.0 / pivot
            done[at] = jnp.where(sub == place + i, lines[i] * lax.rsqrt(pivot), done[at])
            scaled = lines[i] * inverse
            for l in range(i + 1, panel):
                entry = jnp.broadcast_to(columns[i][0][place + l:place + l + 1], wide)
                ratio = entry * inverse
                lines[l] = lines[l] - entry * scaled
                columns[l] = [one - two * ratio for one, two in zip(columns[l], columns[i])]
            lines[i] = scaled
        for t in below:
            take = sum(columns[i][t - at] * lines[i] for i in range(panel))
            rows[t] = rows[t] - (jnp.where(sub >= place + panel, take, 0.0) if t == at else take)
    return pltpu.roll(jnp.concatenate(done), half, 1)


def partials_of(narrow, recv, block, refs):
    ring = recv.shape[0]
    rank = narrow.shape[0]
    square = dot(narrow, narrow, ((1,), (1,)))
    for ref in refs:
        ref[:, ring * block:] = jnp.zeros((rank, LANES), jnp.float32)
        ref[:, ring * block:ring * block + rank] = square
    for j in range(ring):
        part = dot(recv[j, :block], narrow, ((1,), (1,))).T
        for ref in refs:
            ref[:, j * block:(j + 1) * block] = part


def totals_of(spot, got, gram, block, ring):
    rank = got.shape[1]
    total = got[0]
    for copy in range(1, got.shape[0]):
        total = total + got[copy]
    wide = total[:, :ring * block]
    gram[...] = total[:, ring * block:]

    @pl.when(spot[1] == 0)
    def _():
        gram[:, :rank] = dot(wide, wide, ((1,), (1,)))

    return wide


def times_matrix(wide, recv, block):
    return dot(wide, recv[:, :block].reshape(-1, block), ((1,), (0,)))


def first_kernel(block, spot, recv, start_query, start_output, sent, narrow, gram):
    @pl.when(spot[1] == 0)
    def _():
        narrow[...] = start_query[...]

    @pl.when(spot[1] == 1)
    def _():
        narrow[...] = times_matrix(start_output[...], recv, block)

    partials_of(narrow[...], recv, block, [sent.at[peer] for peer in range(sent.shape[0])])


def middle_kernel(block, spot, recv, got, sent, narrow, gram, stage, sems):
    ring = recv.shape[0]
    rank = got.shape[1]
    wide = totals_of(spot, got, gram, block, ring)
    plain = times_matrix(wide, recv, block)
    onward = [dot(plain, recv[j, :block], ((1,), (1,))) for j in range(ring)]
    inverse = invert_lower(gram[...])[:, :rank]
    value = dot(inverse, plain, ((1,), (0,)))
    narrow[...] = value
    half = ring // 2 * block
    parts = slice(0, half), slice(half, stage.shape[1])
    copies = [
        pltpu.make_async_copy(stage.at[:, part], sent.at[peer, :, part], sems.at[n, peer])
        for n, part in enumerate(parts) for peer in range(sent.shape[0])
    ]
    peers = sent.shape[0]
    stage[:, parts[0]] = dot(inverse, jnp.concatenate(onward[:ring // 2], axis=1), ((1,), (0,)))
    for copy in copies[:peers]:
        copy.start()
    stage[:, half:ring * block] = dot(inverse, jnp.concatenate(onward[ring // 2:], axis=1), ((1,), (0,)))
    stage[:, ring * block:] = jnp.zeros((rank, LANES), jnp.float32)
    stage[:, ring * block:ring * block + rank] = dot(value, value, ((1,), (1,)))
    for copy in copies[peers:]:
        copy.start()
    for copy in copies:
        copy.wait()


def last_kernel(block, spot, recv, got, narrow, factors, gram):
    ring = recv.shape[0]
    rank = got.shape[1]
    wide = totals_of(spot, got, gram, block, ring)
    plain = jnp.where(spot[1] == 0, times_matrix(wide, recv, block), narrow[...])
    inverse = invert_lower(gram[...])[:, :rank]
    factors[:, :ring * block] = dot(inverse, wide, ((1,), (0,)))
    factors[:, ring * block:] = dot(inverse, plain, ((1,), (0,)))


def final_kernel(block, shards, earlier, spot, *refs):
    refs = refs[earlier:]
    old, factors, grad_query, error_query, grad_output, error_output, moment_query, moment_output = refs[:8]
    (new_error_query, new_error_output, new_moment_query, new_moment_output, new_weight_query, new_weight_output) = refs[8:14]
    error_q, error_o, weight_q, weight_o, moment, kept, sems = refs[14:]
    height, width = error_query.shape
    rows = moment_query.shape[0]
    ring = height // block
    scale = 1.0 / shards
    load = pltpu.make_async_copy(old, kept, sems.at[2, 0])
    load.start()
    narrow = factors[:, height:] * scale

    def change():
        along = spot[0] * rows
        base = pl.multiple_of(along // LANES * LANES, LANES)
        picked = pltpu.roll(factors[:, pl.ds(base, LANES)], (LANES - along % LANES) % LANES, 1)
        return dot(picked, narrow, ((0,), (0,)))[:rows]

    def parts(j):
        down = pl.ds(j * block, block)
        return down, slice(j * block, (j + 1) * block)

    @pl.when(spot[1] == 0)
    def _():
        copies = [pltpu.make_async_copy(moment, new_moment_query, sems.at[2, 1])]
        for start in (0, ring // 2):
            for j in range(start, start + ring // 2):
                at, down = parts(j)
                approx = dot(factors[:, down], narrow, ((0,), (0,)))
                error_q[down] = grad_query[down].astype(jnp.float32) + error_query[down] - approx
                weight_q[down] = -0.01 * approx
                copies.append(pltpu.make_async_copy(error_q.at[at], new_error_query.at[at], sems.at[0, j]))
                copies[-1].start()
            if start == 0:
                moment[...] = 0.9 * moment_query[...] + change()
                copies[0].start()
                load.wait()
            for j in range(start, start + ring // 2):
                at, down = parts(j)
                weight_q[down] = kept[down] + weight_q[down]
                copies.append(pltpu.make_async_copy(weight_q.at[at], new_weight_query.at[at], sems.at[1, j]))
                copies[-1].start()
        for copy in copies:
            copy.wait()

    @pl.when(spot[1] == 1)
    def _():
        copies = [pltpu.make_async_copy(moment, new_moment_output, sems.at[2, 1])]
        for start in (0, ring // 2):
            for j in range(start, start + ring // 2):
                at, down = parts(j)
                approx = dot(narrow, factors[:, down], ((0,), (0,)))
                error_o[:, down] = grad_output[:, down].astype(jnp.float32) + error_output[:, down] - approx
                weight_o[:, down] = -0.01 * approx
                copies.append(pltpu.make_async_copy(error_o.at[:, at], new_error_output.at[:, at], sems.at[0, j]))
                copies[-1].start()
            if start == 0:
                moment[...] = 0.9 * moment_output[...] + change()
                copies[0].start()
                load.wait()
            for j in range(start, start + ring // 2):
                at, down = parts(j)
                weight_o[:, down] = kept[down] + weight_o[:, down]
                copies.append(pltpu.make_async_copy(weight_o.at[:, at], new_weight_output.at[:, at], sems.at[1, j]))
                copies[-1].start()
        for copy in copies:
            copy.wait()


def prelude_kernel(ring, per, slot, vec, spot, *refs):
    far, total, near, (line, sems, big) = refs[:11], refs[11], refs[12:23], refs[23:]
    moves = [pltpu.make_async_copy(far[n], near[n], sems.at[n]) for n in range(4, 11)]
    grad_q, error_q, grad_o, error_o, grad_vector, weight_query, moment_query, weight_output, moment_output = near[:9]
    weight_vector, moment_vector = near[9:]
    height, width = grad_q.shape
    block = height // ring
    tall = block + slot
    rows = weight_query.shape[0]
    small = weight_vector.shape[1]
    index, which = spot[0], spot[1]

    span = ring // 2 * block // max(ring // 4, 1)
    pieces = [pl.ds(n * span, span) for n in range(height // span)]
    down = [[pltpu.make_async_copy(far[a].at[p], near[a].at[p], big.at[a, n]) for a in (0, 1)] for n, p in enumerate(pieces)]
    across = [
        [pltpu.make_async_copy(far[a].at[:, p], near[a].at[:, p], big.at[a - 2, n]) for a in (2, 3)]
        for n, p in enumerate(pieces)
    ]

    @pl.when(which == 0)
    def _():
        for pair in down:
            for move in pair:
                move.start()

    @pl.when(which == 1)
    def _():
        for pair in across:
            for move in pair:
                move.start()

    for move in moves:
        move.start()
    for move in moves:
        move.wait()
    line[...] = jnp.zeros_like(line)
    line[0:1, :small] = weight_vector[...] - 0.009 * moment_vector[...]
    first = index * small
    spread = pltpu.roll(jnp.broadcast_to(line[0:1], (slot, LANES)), first % LANES, 1)
    sub = lax.broadcasted_iota(jnp.int32, (slot, LANES), 0)
    lane = lax.broadcasted_iota(jnp.int32, (slot, LANES), 1)
    for j in range(ring):
        after = LANES * (per * j + sub - per) + lane - first
        inside = (sub >= per) & (sub < 2 * per) & (after >= 0) & (after < small)
        total[j * tall + block:(j + 1) * tall] = jnp.where(inside, spread, 0.0)
        for n in range(per):
            r = per * j + n
            if r * LANES < vec:
                row = grad_vector[:, r * LANES:(r + 1) * LANES].astype(jnp.float32)
                total[j * tall + block + n:j * tall + block + n + 1] = row

    @pl.when(which == 0)
    def _():
        total[ring * tall:] = weight_query[...] - 0.009 * moment_query[...]
        for j in range(ring):
            if j * block % span == 0:
                for move in down[j * block // span]:
                    move.wait()
            at = slice(j * block, (j + 1) * block)
            total[j * tall:j * tall + block] = grad_q[at].astype(jnp.float32) + error_q[at]

    @pl.when(which == 1)
    def _():
        total[ring * tall:] = weight_output[...] - 0.009 * moment_output[...]
        for j in range(ring):
            if j * block % span == 0:
                for move in across[j * block // span]:
                    move.wait()
            at = slice(j * block, (j + 1) * block)
            total[j * tall:j * tall + block] = grad_o[:, at].astype(jnp.float32) + error_o[:, at]


def vector_kernel(block, per, shards, spot, recv, moment_vector, new_moment, new_weight, mean, kept):
    ring = recv.shape[0]
    small = moment_vector.shape[1]
    for j in range(ring):
        mean[per * j:per * (j + 1)] = recv[j, block:block + per] * (1.0 / shards)
        kept[per * j:per * (j + 1)] = recv[j, block + per:block + 2 * per]
    mean[per * ring:] = jnp.zeros((mean.shape[0] - per * ring, LANES), jnp.float32)
    lines = new_weight.shape[0]
    new_weight[...] = kept[:lines] - 0.01 * mean[:lines]
    first = spot[0] * small
    row, off = first // LANES, first % LANES
    shift = (LANES - off) % LANES
    one = pltpu.roll(jnp.broadcast_to(mean[pl.ds(row, 1)], (8, LANES)), shift, 1)
    two = pltpu.roll(jnp.broadcast_to(mean[pl.ds(row + 1, 1)], (8, LANES)), shift, 1)
    lane = lax.broadcasted_iota(jnp.int32, (8, LANES), 1)
    own = jnp.where(lane < LANES - off, one, two)
    new_moment[...] = 0.9 * moment_vector[...] + own[0:1, :small]


def shape(*dims):
    return jax.ShapeDtypeStruct(dims, jnp.float32)


def run(kernel, given, out_shape, scratch, out_specs=None, outside=0, **options):
    whole = pl.BlockSpec(memory_space=pltpu.VMEM)
    left = [pl.BlockSpec(memory_space=pltpu.HBM)] * outside
    specs = [pl.BlockSpec(memory_space=pltpu.SMEM)] + left + [whole] * (len(given) - 1 - outside)
    if out_specs is None:
        out_specs = jax.tree.map(lambda _: whole, out_shape)
    return pl.pallas_call(
        kernel, out_shape=out_shape, in_specs=specs, out_specs=out_specs, scratch_shapes=scratch,
        compiler_params=pltpu.CompilerParams(vmem_limit_bytes=40 * 2**20), **options,
    )(*given)


def local(
    grad_query,
    error_query,
    grad_output,
    error_output,
    start_query,
    start_output,
    weight_query,
    weight_output,
    moment_query,
    moment_output,
    grad_vector,
    moment_vector,
    weight_vector,
):
    shards = lax.axis_size("shard")
    tensors = lax.axis_size("tensor")
    index = lax.axis_index("shard")
    ring = ring_size(shards)
    first, second = groups(ring)
    asks = (index % 2) == 1
    width = start_query.shape[0]
    height = start_output.shape[0]
    rank = start_query.shape[1]
    block = height // ring
    rows = height // shards
    vec = grad_vector.shape[1]
    small = vec // shards
    lines = vec // LANES
    per = -(-lines // ring)
    slot = -(-2 * per // 8) * 8
    tall = block + slot
    assert width == LANES and rows * shards == height and small * shards == vec and lines * LANES == vec

    spot = jnp.stack([index, 1 - index % 2]).astype(jnp.int32)
    given = (
        grad_query[0], error_query[0], grad_output[0], error_output[0], grad_vector, weight_query, moment_query,
        weight_output.T, moment_output.T, weight_vector[None], moment_vector[None],
    )
    given = [pltpu.with_memory_space_constraint(value, pltpu.HBM) for value in given]

    def prelude(spot):
        return run(
            functools.partial(prelude_kernel, ring, per, slot, vec), (spot, *given), shape(ring * tall + rows, LANES),
            [
                *(pltpu.VMEM(value.shape, value.dtype) for value in given),
                pltpu.VMEM((8, LANES), jnp.float32), pltpu.SemaphoreType.DMA((len(given),)),
                pltpu.SemaphoreType.DMA((2, ring)),
            ],
            outside=len(given),
        )

    swapped = jnp.stack([index, index % 2]).astype(jnp.int32)
    got = swap_cores(prelude(swapped), shards)
    mine = prelude(spot)
    summed = (mine[:ring * tall] + got[:ring * tall]).reshape(ring, tall, LANES)
    own_kept, got_kept = mine[ring * tall:], got[ring * tall:]
    pair_kept = jnp.where(asks, jnp.concatenate([got_kept, own_kept]), jnp.concatenate([own_kept, got_kept]))
    summed, pair_kept = lax.optimization_barrier((summed, pair_kept))

    part = exchange(summed, first).sum(0)
    every = share(jnp.concatenate([part, pair_kept]), second, ring)
    whole = every[:, :tall].sum(0)
    square = jnp.where(asks, whole[:block], whole[:block].T)
    kept_rows = every[:, tall:].reshape(block, LANES)
    every = share(jnp.concatenate([square, whole[block:], kept_rows]), first, ring)

    gram = pltpu.VMEM((rank, LANES), jnp.float32)
    partials = shape(tensors, rank, height + LANES)

    def gathered(value):
        return lax.all_to_all(value, "tensor", 0, 0, tiled=True)

    stage = [pltpu.VMEM((rank, height + LANES), jnp.float32), pltpu.SemaphoreType.DMA((2, tensors))]
    outside, within = pl.BlockSpec(memory_space=pl.ANY), pl.BlockSpec(memory_space=pltpu.VMEM)
    sent, narrow = run(
        functools.partial(first_kernel, block), (spot, every, start_query.T, start_output.T),
        (partials, shape(rank, width)), [gram],
    )
    for turn in range(ROUNDS - 1):
        sent, narrow = run(
            functools.partial(middle_kernel, block), (spot, every, gathered(sent)), (partials, shape(rank, width)),
            [gram, *stage], (outside, within),
        )

    sent, every = lax.optimization_barrier((sent, every))
    kept_all = every[:, tall:].reshape(ring, ring, 2 * rows, LANES)
    kept_turned = kept_all.transpose(1, 0, 2, 3).reshape(ring, block, LANES).transpose(0, 2, 1)
    kept_all = jnp.where(asks, kept_all.reshape(ring, block, LANES), kept_turned).reshape(height, LANES)
    kept_other = swap_cores(kept_all, shards)
    new_moment_vector, new_weight_vector = run(
        functools.partial(vector_kernel, block, per, shards), (spot, every, moment_vector[None]),
        (shape(1, small), shape(lines, LANES)),
        [pltpu.VMEM((per * ring + 8, LANES), jnp.float32), pltpu.VMEM((per * ring, LANES), jnp.float32)],
    )
    got, new_moment_vector, new_weight_vector = lax.optimization_barrier(
        (gathered(sent), new_moment_vector, new_weight_vector)
    )
    mine = run(functools.partial(last_kernel, block), (spot, every, got, narrow), shape(rank, height + width), [gram])
    other = swap_cores(mine, shards)
    big = [pltpu.VMEM((height, width), jnp.float32), pltpu.VMEM((width, height), jnp.float32)]
    ends = (shape(height, width), shape(width, height), shape(rows, width), shape(rows, width), shape(height, width), shape(width, height))
    local_ones = (grad_query[0], error_query[0], grad_output[0], error_output[0], moment_query, moment_output.T)

    def final(spot, before, kept, factors):
        return run(
            functools.partial(final_kernel, block, shards, len(before)), (spot, *before, kept, factors, *local_ones), ends,
            [*big, *big, pltpu.VMEM((rows, width), jnp.float32), big[0], pltpu.SemaphoreType.DMA((3, ring))],
            (outside,) * 6, len(before) + 1, input_output_aliases={n + 1: n for n in range(len(before))},
        )

    ends_of_mine = final(spot, (), kept_all, mine)
    (
        new_error_query, new_error_output, new_moment_query, new_moment_output, new_weight_query, new_weight_output,
    ) = final(swapped, ends_of_mine, kept_other, other)
    new_error_query = new_error_query[None]
    new_error_output = new_error_output[None]
    new_moment_output = new_moment_output.T
    return (
        new_error_query,
        new_error_output,
        new_moment_query,
        new_moment_output,
        new_weight_query,
        new_weight_output,
        new_moment_vector[0],
        new_weight_vector.reshape(vec),
    )


def solution(mesh):
    in_specs = (
        P("shard", None, "tensor"),
        P("shard", None, "tensor"),
        P("shard", "tensor", None),
        P("shard", "tensor", None),
        P("tensor", None),
        P(),
        P("shard", "tensor"),
        P("tensor", "shard"),
        P("shard", "tensor"),
        P("tensor", "shard"),
        P("shard", None),
        P("shard"),
        P("shard"),
    )
    out_specs = (
        P("shard", None, "tensor"),
        P("shard", "tensor", None),
        P("shard", "tensor"),
        P("tensor", "shard"),
        P(None, "tensor"),
        P("tensor", None),
        P("shard"),
        P(),
    )
    return jax.shard_map(local, mesh=mesh, in_specs=in_specs, out_specs=out_specs, check_vma=False)
```

```python
import functools

import jax
import jax.numpy as jnp
from jax import lax
from jax.experimental import pallas as pl
from jax.experimental.pallas import tpu as pltpu
from jax.sharding import PartitionSpec as P

ROUNDS = 2
LANES = 128

highest = lax.Precision.HIGHEST


def dot(left, right, dims):
    return lax.dot_general(left, right, (dims, ((), ())), precision=highest, preferred_element_type=jnp.float32)


def ring_size(shards):
    ring = int(round((shards // 2) ** 0.5))
    assert 2 * ring * ring == shards
    return ring


def groups(ring):
    along_y = [[[(2 * (ring * y + z)) + c for y in range(ring)] for z in range(ring)] for c in range(2)]
    along_z = [[[(2 * (ring * y + z)) + c for z in range(ring)] for y in range(ring)] for c in range(2)]
    return along_z[0] + along_y[1], along_y[0] + along_z[1]


def swap_cores(value, shards):
    return lax.ppermute(value, "shard", [(s, s ^ 1) for s in range(shards)])


def exchange(value, group):
    return lax.all_to_all(value, "shard", 0, 0, axis_index_groups=group, tiled=True)


def share(value, group, size):
    return exchange(jnp.broadcast_to(value[None], (size, *value.shape)), group)


def invert_lower(gram):
    rank = gram.shape[0]
    tiles = rank // 8
    half = LANES // 2
    lane = lax.broadcasted_iota(jnp.int32, (8, LANES), 1)
    sub = lax.broadcasted_iota(jnp.int32, (8, LANES), 0)
    rows = [
        jnp.where(lane < rank, gram[8 * t:8 * t + 8], jnp.where(lane == sub + (8 * t + half), 1.0, 0.0))
        for t in range(tiles)
    ]
    done = [jnp.zeros((8, LANES), jnp.float32) for _ in range(tiles)]
    wide = (8, LANES)
    panel = 8
    for k in range(0, rank, panel):
        at, place = k // 8, k % 8
        below = range(at, tiles)
        columns = [[jnp.broadcast_to(rows[t][:, k + i:k + i + 1], wide) for t in below] for i in range(panel)]
        lines = [jnp.broadcast_to(rows[at][place + i:place + i + 1], wide) for i in range(panel)]
        for i in range(panel):
            pivot = jnp.broadcast_to(columns[i][0][place + i:place + i + 1], wide)
            inverse = 1.0 / pivot
            done[at] = jnp.where(sub == place + i, lines[i] * lax.rsqrt(pivot), done[at])
            scaled = lines[i] * inverse
            for l in range(i + 1, panel):
                entry = jnp.broadcast_to(columns[i][0][place + l:place + l + 1], wide)
                ratio = entry * inverse
                lines[l] = lines[l] - entry * scaled
                columns[l] = [one - two * ratio for one, two in zip(columns[l], columns[i])]
            lines[i] = scaled
        for t in below:
            take = sum(columns[i][t - at] * lines[i] for i in range(panel))
            rows[t] = rows[t] - (jnp.where(sub >= place + panel, take, 0.0) if t == at else take)
    return pltpu.roll(jnp.concatenate(done), half, 1)


def partials_of(narrow, recv, block, refs):
    ring = recv.shape[0]
    rank = narrow.shape[0]
    square = dot(narrow, narrow, ((1,), (1,)))
    for ref in refs:
        ref[:, ring * block:] = jnp.zeros((rank, LANES), jnp.float32)
        ref[:, ring * block:ring * block + rank] = square
    for j in range(ring):
        part = dot(recv[j, :block], narrow, ((1,), (1,))).T
        for ref in refs:
            ref[:, j * block:(j + 1) * block] = part


def totals_of(spot, got, gram, block, ring):
    rank = got.shape[1]
    total = got[0]
    for copy in range(1, got.shape[0]):
        total = total + got[copy]
    wide = total[:, :ring * block]
    gram[...] = total[:, ring * block:]

    @pl.when(spot[1] == 0)
    def _():
        gram[:, :rank] = dot(wide, wide, ((1,), (1,)))

    return wide


def times_matrix(wide, recv, block):
    return dot(wide, recv[:, :block].reshape(-1, block), ((1,), (0,)))


def first_kernel(block, spot, recv, start_query, start_output, sent, narrow, gram):
    @pl.when(spot[1] == 0)
    def _():
        narrow[...] = start_query[...]

    @pl.when(spot[1] == 1)
    def _():
        narrow[...] = times_matrix(start_output[...], recv, block)

    partials_of(narrow[...], recv, block, [sent.at[peer] for peer in range(sent.shape[0])])


def middle_kernel(block, spot, recv, got, sent, narrow, gram, stage, sems):
    ring = recv.shape[0]
    rank = got.shape[1]
    wide = totals_of(spot, got, gram, block, ring)
    plain = times_matrix(wide, recv, block)
    onward = [dot(plain, recv[j, :block], ((1,), (1,))) for j in range(ring)]
    inverse = invert_lower(gram[...])[:, :rank]
    value = dot(inverse, plain, ((1,), (0,)))
    narrow[...] = value
    half = ring // 2 * block
    parts = slice(0, half), slice(half, stage.shape[1])
    copies = [
        pltpu.make_async_copy(stage.at[:, part], sent.at[peer, :, part], sems.at[n, peer])
        for n, part in enumerate(parts) for peer in range(sent.shape[0])
    ]
    peers = sent.shape[0]
    stage[:, parts[0]] = dot(inverse, jnp.concatenate(onward[:ring // 2], axis=1), ((1,), (0,)))
    for copy in copies[:peers]:
        copy.start()
    stage[:, half:ring * block] = dot(inverse, jnp.concatenate(onward[ring // 2:], axis=1), ((1,), (0,)))
    stage[:, ring * block:] = jnp.zeros((rank, LANES), jnp.float32)
    stage[:, ring * block:ring * block + rank] = dot(value, value, ((1,), (1,)))
    for copy in copies[peers:]:
        copy.start()
    for copy in copies:
        copy.wait()


def last_kernel(block, spot, recv, got, narrow, factors, gram):
    ring = recv.shape[0]
    rank = got.shape[1]
    wide = totals_of(spot, got, gram, block, ring)
    plain = jnp.where(spot[1] == 0, times_matrix(wide, recv, block), narrow[...])
    inverse = invert_lower(gram[...])[:, :rank]
    factors[:, :ring * block] = dot(inverse, wide, ((1,), (0,)))
    factors[:, ring * block:] = dot(inverse, plain, ((1,), (0,)))


def final_kernel(block, shards, earlier, spot, *refs):
    refs = refs[earlier:]
    old, factors, grad_query, error_query, grad_output, error_output, moment_query, moment_output = refs[:8]
    (new_error_query, new_error_output, new_moment_query, new_moment_output, new_weight_query, new_weight_output) = refs[8:14]
    error_q, error_o, weight_q, weight_o, moment, kept, sems = refs[14:]
    height, width = error_query.shape
    rows = moment_query.shape[0]
    ring = height // block
    scale = 1.0 / shards
    load = pltpu.make_async_copy(old, kept, sems.at[2, 0])
    load.start()
    narrow = factors[:, height:] * scale

    def change():
        along = spot[0] * rows
        base = pl.multiple_of(along // LANES * LANES, LANES)
        picked = pltpu.roll(factors[:, pl.ds(base, LANES)], (LANES - along % LANES) % LANES, 1)
        return dot(picked, narrow, ((0,), (0,)))[:rows]

    def parts(j):
        down = pl.ds(j * block, block)
        return down, slice(j * block, (j + 1) * block)

    @pl.when(spot[1] == 0)
    def _():
        copies = []
        for j in range(ring):
            at, down = parts(j)
            approx = dot(factors[:, down], narrow, ((0,), (0,)))
            error_q[down] = grad_query[down].astype(jnp.float32) + error_query[down] - approx
            weight_q[down] = -0.01 * approx
            copies.append(pltpu.make_async_copy(error_q.at[at], new_error_query.at[at], sems.at[0, j]))
            copies[-1].start()
        moment[...] = 0.9 * moment_query[...] + change()
        copies.append(pltpu.make_async_copy(moment, new_moment_query, sems.at[2, 1]))
        copies[-1].start()
        load.wait()
        for j in range(ring):
            at, down = parts(j)
            weight_q[down] = kept[down] + weight_q[down]
            copies.append(pltpu.make_async_copy(weight_q.at[at], new_weight_query.at[at], sems.at[1, j]))
            copies[-1].start()
        for copy in copies:
            copy.wait()

    @pl.when(spot[1] == 1)
    def _():
        copies = []
        for j in range(ring):
            at, down = parts(j)
            approx = dot(narrow, factors[:, down], ((0,), (0,)))
            error_o[:, down] = grad_output[:, down].astype(jnp.float32) + error_output[:, down] - approx
            weight_o[:, down] = -0.01 * approx
            copies.append(pltpu.make_async_copy(error_o.at[:, at], new_error_output.at[:, at], sems.at[0, j]))
            copies[-1].start()
        moment[...] = 0.9 * moment_output[...] + change()
        copies.append(pltpu.make_async_copy(moment, new_moment_output, sems.at[2, 1]))
        copies[-1].start()
        load.wait()
        for j in range(ring):
            at, down = parts(j)
            weight_o[:, down] = kept[down] + weight_o[:, down]
            copies.append(pltpu.make_async_copy(weight_o.at[:, at], new_weight_output.at[:, at], sems.at[1, j]))
            copies[-1].start()
        for copy in copies:
            copy.wait()


def prelude_kernel(ring, per, slot, vec, spot, *refs):
    far, total, near, (line, sems) = refs[:11], refs[11], refs[12:23], refs[23:]
    moves = [pltpu.make_async_copy(*pair, sems.at[n]) for n, pair in enumerate(zip(far, near))]
    grad_q, error_q, grad_o, error_o, grad_vector, weight_query, moment_query, weight_output, moment_output = near[:9]
    weight_vector, moment_vector = near[9:]
    height, width = grad_q.shape
    block = height // ring
    tall = block + slot
    rows = weight_query.shape[0]
    small = weight_vector.shape[1]
    index, which = spot[0], spot[1]

    @pl.when(which == 0)
    def _():
        moves[0].start()
        moves[1].start()

    @pl.when(which == 1)
    def _():
        moves[2].start()
        moves[3].start()

    for move in moves[4:]:
        move.start()
    for move in moves[4:]:
        move.wait()
    line[...] = jnp.zeros_like(line)
    line[0:1, :small] = weight_vector[...] - 0.009 * moment_vector[...]
    first = index * small
    spread = pltpu.roll(jnp.broadcast_to(line[0:1], (slot, LANES)), first % LANES, 1)
    sub = lax.broadcasted_iota(jnp.int32, (slot, LANES), 0)
    lane = lax.broadcasted_iota(jnp.int32, (slot, LANES), 1)
    for j in range(ring):
        after = LANES * (per * j + sub - per) + lane - first
        inside = (sub >= per) & (sub < 2 * per) & (after >= 0) & (after < small)
        total[j * tall + block:(j + 1) * tall] = jnp.where(inside, spread, 0.0)
        for n in range(per):
            r = per * j + n
            if r * LANES < vec:
                row = grad_vector[:, r * LANES:(r + 1) * LANES].astype(jnp.float32)
                total[j * tall + block + n:j * tall + block + n + 1] = row

    @pl.when(which == 0)
    def _():
        total[ring * tall:] = weight_query[...] - 0.009 * moment_query[...]
        moves[0].wait()
        moves[1].wait()
        for j in range(ring):
            down = slice(j * block, (j + 1) * block)
            total[j * tall:j * tall + block] = grad_q[down].astype(jnp.float32) + error_q[down]

    @pl.when(which == 1)
    def _():
        total[ring * tall:] = weight_output[...] - 0.009 * moment_output[...]
        moves[2].wait()
        moves[3].wait()
        for j in range(ring):
            down = slice(j * block, (j + 1) * block)
            total[j * tall:j * tall + block] = grad_o[:, down].astype(jnp.float32) + error_o[:, down]


def vector_kernel(block, per, shards, spot, recv, moment_vector, new_moment, new_weight, mean, kept):
    ring = recv.shape[0]
    small = moment_vector.shape[1]
    for j in range(ring):
        mean[per * j:per * (j + 1)] = recv[j, block:block + per] * (1.0 / shards)
        kept[per * j:per * (j + 1)] = recv[j, block + per:block + 2 * per]
    mean[per * ring:] = jnp.zeros((mean.shape[0] - per * ring, LANES), jnp.float32)
    lines = new_weight.shape[0]
    new_weight[...] = kept[:lines] - 0.01 * mean[:lines]
    first = spot[0] * small
    row, off = first // LANES, first % LANES
    shift = (LANES - off) % LANES
    one = pltpu.roll(jnp.broadcast_to(mean[pl.ds(row, 1)], (8, LANES)), shift, 1)
    two = pltpu.roll(jnp.broadcast_to(mean[pl.ds(row + 1, 1)], (8, LANES)), shift, 1)
    lane = lax.broadcasted_iota(jnp.int32, (8, LANES), 1)
    own = jnp.where(lane < LANES - off, one, two)
    new_moment[...] = 0.9 * moment_vector[...] + own[0:1, :small]


def shape(*dims):
    return jax.ShapeDtypeStruct(dims, jnp.float32)


def run(kernel, given, out_shape, scratch, out_specs=None, outside=0, **options):
    whole = pl.BlockSpec(memory_space=pltpu.VMEM)
    left = [pl.BlockSpec(memory_space=pltpu.HBM)] * outside
    specs = [pl.BlockSpec(memory_space=pltpu.SMEM)] + left + [whole] * (len(given) - 1 - outside)
    if out_specs is None:
        out_specs = jax.tree.map(lambda _: whole, out_shape)
    return pl.pallas_call(
        kernel, out_shape=out_shape, in_specs=specs, out_specs=out_specs, scratch_shapes=scratch,
        compiler_params=pltpu.CompilerParams(vmem_limit_bytes=40 * 2**20), **options,
    )(*given)


def local(
    grad_query,
    error_query,
    grad_output,
    error_output,
    start_query,
    start_output,
    weight_query,
    weight_output,
    moment_query,
    moment_output,
    grad_vector,
    moment_vector,
    weight_vector,
):
    shards = lax.axis_size("shard")
    tensors = lax.axis_size("tensor")
    index = lax.axis_index("shard")
    ring = ring_size(shards)
    first, second = groups(ring)
    asks = (index % 2) == 1
    width = start_query.shape[0]
    height = start_output.shape[0]
    rank = start_query.shape[1]
    block = height // ring
    rows = height // shards
    vec = grad_vector.shape[1]
    small = vec // shards
    lines = vec // LANES
    per = -(-lines // ring)
    slot = -(-2 * per // 8) * 8
    tall = block + slot
    assert width == LANES and rows * shards == height and small * shards == vec and lines * LANES == vec

    spot = jnp.stack([index, 1 - index % 2]).astype(jnp.int32)
    given = (
        grad_query[0], error_query[0], grad_output[0], error_output[0], grad_vector, weight_query, moment_query,
        weight_output.T, moment_output.T, weight_vector[None], moment_vector[None],
    )
    given = [pltpu.with_memory_space_constraint(value, pltpu.HBM) for value in given]

    def prelude(spot):
        return run(
            functools.partial(prelude_kernel, ring, per, slot, vec), (spot, *given), shape(ring * tall + rows, LANES),
            [
                *(pltpu.VMEM(value.shape, value.dtype) for value in given),
                pltpu.VMEM((8, LANES), jnp.float32), pltpu.SemaphoreType.DMA((len(given),)),
            ],
            outside=len(given),
        )

    swapped = jnp.stack([index, index % 2]).astype(jnp.int32)
    got = swap_cores(prelude(swapped), shards)
    mine = prelude(spot)
    summed = (mine[:ring * tall] + got[:ring * tall]).reshape(ring, tall, LANES)
    own_kept, got_kept = mine[ring * tall:], got[ring * tall:]
    pair_kept = jnp.where(asks, jnp.concatenate([got_kept, own_kept]), jnp.concatenate([own_kept, got_kept]))
    summed, pair_kept = lax.optimization_barrier((summed, pair_kept))

    part = exchange(summed, first).sum(0)
    every = share(jnp.concatenate([part, pair_kept]), second, ring)
    whole = every[:, :tall].sum(0)
    square = jnp.where(asks, whole[:block], whole[:block].T)
    kept_rows = every[:, tall:].reshape(block, LANES)
    every = share(jnp.concatenate([square, whole[block:], kept_rows]), first, ring)

    gram = pltpu.VMEM((rank, LANES), jnp.float32)
    partials = shape(tensors, rank, height + LANES)

    def gathered(value):
        return lax.all_to_all(value, "tensor", 0, 0, tiled=True)

    stage = [pltpu.VMEM((rank, height + LANES), jnp.float32), pltpu.SemaphoreType.DMA((2, tensors))]
    outside, within = pl.BlockSpec(memory_space=pl.ANY), pl.BlockSpec(memory_space=pltpu.VMEM)
    sent, narrow = run(
        functools.partial(first_kernel, block), (spot, every, start_query.T, start_output.T),
        (partials, shape(rank, width)), [gram],
    )
    for turn in range(ROUNDS - 1):
        sent, narrow = run(
            functools.partial(middle_kernel, block), (spot, every, gathered(sent)), (partials, shape(rank, width)),
            [gram, *stage], (outside, within),
        )

    sent, every = lax.optimization_barrier((sent, every))
    kept_all = every[:, tall:].reshape(ring, ring, 2 * rows, LANES)
    kept_turned = kept_all.transpose(1, 0, 2, 3).reshape(ring, block, LANES).transpose(0, 2, 1)
    kept_all = jnp.where(asks, kept_all.reshape(ring, block, LANES), kept_turned).reshape(height, LANES)
    kept_other = swap_cores(kept_all, shards)
    new_moment_vector, new_weight_vector = run(
        functools.partial(vector_kernel, block, per, shards), (spot, every, moment_vector[None]),
        (shape(1, small), shape(lines, LANES)),
        [pltpu.VMEM((per * ring + 8, LANES), jnp.float32), pltpu.VMEM((per * ring, LANES), jnp.float32)],
    )
    got, new_moment_vector, new_weight_vector = lax.optimization_barrier(
        (gathered(sent), new_moment_vector, new_weight_vector)
    )
    mine = run(functools.partial(last_kernel, block), (spot, every, got, narrow), shape(rank, height + width), [gram])
    other = swap_cores(mine, shards)
    big = [pltpu.VMEM((height, width), jnp.float32), pltpu.VMEM((width, height), jnp.float32)]
    ends = (shape(height, width), shape(width, height), shape(rows, width), shape(rows, width), shape(height, width), shape(width, height))
    local_ones = (grad_query[0], error_query[0], grad_output[0], error_output[0], moment_query, moment_output.T)

    def final(spot, before, kept, factors):
        return run(
            functools.partial(final_kernel, block, shards, len(before)), (spot, *before, kept, factors, *local_ones), ends,
            [*big, *big, pltpu.VMEM((rows, width), jnp.float32), big[0], pltpu.SemaphoreType.DMA((3, ring))],
            (outside,) * 6, len(before) + 1, input_output_aliases={n + 1: n for n in range(len(before))},
        )

    ends_of_mine = final(spot, (), kept_all, mine)
    (
        new_error_query, new_error_output, new_moment_query, new_moment_output, new_weight_query, new_weight_output,
    ) = final(swapped, ends_of_mine, kept_other, other)
    new_error_query = new_error_query[None]
    new_error_output = new_error_output[None]
    new_moment_output = new_moment_output.T
    return (
        new_error_query,
        new_error_output,
        new_moment_query,
        new_moment_output,
        new_weight_query,
        new_weight_output,
        new_moment_vector[0],
        new_weight_vector.reshape(vec),
    )


def solution(mesh):
    in_specs = (
        P("shard", None, "tensor"),
        P("shard", None, "tensor"),
        P("shard", "tensor", None),
        P("shard", "tensor", None),
        P("tensor", None),
        P(),
        P("shard", "tensor"),
        P("tensor", "shard"),
        P("shard", "tensor"),
        P("tensor", "shard"),
        P("shard", None),
        P("shard"),
        P("shard"),
    )
    out_specs = (
        P("shard", None, "tensor"),
        P("shard", "tensor", None),
        P("shard", "tensor"),
        P("tensor", "shard"),
        P(None, "tensor"),
        P("tensor", None),
        P("shard"),
        P(),
    )
    return jax.shard_map(local, mesh=mesh, in_specs=in_specs, out_specs=out_specs, check_vma=False)
```
